256 devices in a mesh: tile: 128 (over y, z, x), nrn: 2 (over core).
Axes of the slice: x: 4, y: 4, z: 8, core: 2. Of those that a mesh axis runs over, the one named last changes fastest.
Arguments:
- movie: bfloat16 [2, 128, 1024, 1024], P('nrn', 'tile'), may hold values from 0.099609375 to 2
- shifts: int32 [2, 128, 2], P('nrn', 'tile'), may hold values from -4 to 4
- footprints: bfloat16 [12288, 16, 128], P('tile'), may hold values from 0.019897461 to 1
- blocks: int32 [12288, 16], P('tile'), may hold values from 0 to 4095, as said below
- traces: float32 [2, 12288, 4], P('nrn', 'tile'), may hold values from 0.1 to 2
- counts: int32 [128], P('tile'), may hold values from 24 to 96, as said below
Outputs:
- new_traces: float32 [2, 12288, 4], P('nrn', 'tile')
- new_footprints: bfloat16 [12288, 16, 128], P('tile')
The draws below stay inside these ranges and needn't reach their ends.
Inputs may be any that keep to these rules, and one draw needn't show every extreme that they name: Each neuron has a plane z < 29, a block row r < 1 and a block column x < 63; blocks[k, 4 a + 2 d + e] = ((z + a) * 2 + r + d) * 64 + x + e for a in 0..3 and d, e in 0..1, so a neuron covers 2 x 2 blocks on each of 4 planes and reaches at most one block row below its tile's rows. `counts`: some tile is full and some holds 24 live neurons in every draw.
All inputs are finite; a program needn't handle non-finite values.
Results may differ from the reference program's by a relative error of at most 0.00105.
Values may be sent and summed in bfloat16 or wider, within the bound.
No kernel may reach another device: no remote copies, remote signals or barrier semaphores. Data moves between devices by JAX's collectives and lax.ppermute only.
A program may use at most 128 MiB of HBM per device.

```python
import math
import jax
import jax.numpy as jnp
from jax import lax

H = 1024
W = 1024
Z = 32
NB = 16
PR = 8
PC = 16
VOX = 128
KT = 96
FH = 4
ZF = 128
PB = 1
RB = 2
XB = 64
TILES = 128
NEURONS = 12288


def draw_blocks(key, part):
    base = jax.random.fold_in(key, 11)
    key_plane, key_row, key_col = jax.random.split(base, 3)
    plane = jax.random.randint(key_plane, (NEURONS,), 0, Z - 3)
    row_start = jax.random.randint(key_row, (NEURONS,), 0, PB)
    column = jax.random.randint(key_col, (NEURONS,), 0, XB - 1)
    plane = plane.at[0].set(Z - 4).at[1].set(0)
    row_start = row_start.at[0].set(PB - 1).at[1].set(0)
    column = column.at[0].set(XB - 2).at[1].set(0)
    slot_index = jnp.arange(NB, dtype=jnp.int32)
    plane_step = slot_index // 4
    row_step = slot_index // 2 % 2
    col_step = slot_index % 2
    planes_all = plane[:, None] + plane_step[None, :]
    rows_all = row_start[:, None] + row_step[None, :]
    cols_all = column[:, None] + col_step[None, :]
    return ((planes_all * RB + rows_all) * XB + cols_all).astype(jnp.int32)


def draw_counts(key, part):
    base = jax.random.fold_in(key, 23)
    key_count, key_order = jax.random.split(base, 2)
    values = jax.random.randint(key_count, (TILES,), KT // 4, KT + 1)
    order = jax.random.permutation(key_order, TILES)
    values = values.at[order[0]].set(KT).at[order[1]].set(KT // 4)
    return values.astype(jnp.int32)


def plant(entries, own_key, low, high):
    longest = entries.shape.index(max(entries.shape))
    spots = []
    for shift in (0, 1):
        where = [jax.random.randint(jax.random.fold_in(own_key, axis), (), 0, length) for axis, length in enumerate(entries.shape)]
        where[longest] = (where[longest] + shift) % entries.shape[longest]
        spots.append(tuple(where))
    return entries.at[spots[0]].set(low).at[spots[1]].set(high)


def steps_of(key, shape, shards, smallest, high):
    def one(position, blocks):
        steps = jax.random.uniform(jax.random.fold_in(jax.random.fold_in(key, 6), position), (blocks,), jnp.float32, smallest / len(shards), high / len(shards))
        return jnp.repeat(jnp.exp(steps), shape[position] // blocks).reshape((-1,) + (1,) * (len(shape) - position - 1))

    factor_of = one(*shards[0])
    for cut in shards[1:]:
        factor_of = factor_of * one(*cut)
    return factor_of


def setup_inputs(seed: int = 0) -> dict:
    key_of = jax.random.split(jax.random.key(seed), 7)
    return {
        "movie": jnp.clip(0.099609375 + 1.9003906 * jax.random.uniform(key_of[0], (2, ZF, H, W), jnp.float32) ** steps_of(key_of[0], (2, ZF, H, W), ((0, 2), (1, 128)), -0.2, 0.2), 0.099609375, 2.0).astype(jnp.bfloat16),
        "shifts": plant(jax.random.randint(key_of[1], (2, ZF, 2), -4, 5), jax.random.fold_in(key_of[1], 1), -4, 4).astype(jnp.int32),
        "footprints": jnp.clip(jnp.exp(math.log(1.0) - 3.9171631 * jax.random.uniform(key_of[2], (NEURONS, NB, VOX), jnp.float32) ** steps_of(key_of[2], (NEURONS, NB, VOX), ((0, 128),), -0.2, 0.2)), 0.019897461, 1.0).astype(jnp.bfloat16),
        "blocks": draw_blocks(jax.random.fold_in(key_of[6], 71), 0),
        "traces": jnp.clip(jnp.exp(math.log(2.0) - 2.9957323 * jax.random.uniform(key_of[4], (2, NEURONS, FH), jnp.float32) ** steps_of(key_of[4], (2, NEURONS, FH), ((0, 2), (1, 128)), -0.2, 0.2)), 0.1, 2.0),
        "counts": draw_counts(jax.random.fold_in(key_of[6], 71), 0),
    }


EPSILON = 1e-6


def register(movie, shifts):
    row_index = jnp.arange(H, dtype=jnp.int32)
    col_index = jnp.arange(W, dtype=jnp.int32)

    def single(picture, offset):
        shifted = jnp.roll(picture, offset[0], axis=0)
        shifted = jnp.roll(shifted, offset[1], axis=1)
        inside_rows = (row_index - offset[0] >= 0) & (row_index - offset[0] < H)
        inside_cols = (col_index - offset[1] >= 0) & (col_index - offset[1] < W)
        inside = inside_rows[:, None] & inside_cols[None, :]
        return jnp.where(inside, shifted, jnp.zeros_like(shifted))

    return jax.vmap(jax.vmap(single))(movie, shifts)


def global_ids(blocks, tile_of):
    plane = blocks // (RB * XB)
    row_in = (blocks // XB) % RB
    column = blocks % XB
    return ((plane * (H // PR + 1) + tile_of[:, None] * PB + row_in) * XB + column).astype(jnp.int32)


def rebuild(masked, trace_all, global_id):
    accumulated = jnp.zeros((Z * (H // PR + 1) * XB, 2, FH, VOX), jnp.float32)

    def scan_step(accumulated, tile_item):
        footprint_tile, trace_tile, tile_ids = tile_item
        contrib = footprint_tile[:, :, None, None, :] * trace_tile[:, None, :, :, None]
        accumulated = accumulated.at[tile_ids.reshape(-1)].add(contrib.reshape(-1, 2, FH, VOX))
        return accumulated, None

    accumulated, _ = lax.scan(scan_step, accumulated,
                              (masked.reshape(TILES, KT, NB, VOX),
                               trace_all.reshape(TILES, KT, 2, FH),
                               global_id.reshape(TILES, KT, NB)))
    return accumulated


def project(recon_field, masked, global_id):
    def single(tile_item):
        footprint_tile, tile_ids = tile_item
        picked = recon_field[tile_ids].astype(jnp.float32)
        return jnp.einsum('kbv,kbpjv->kpj', footprint_tile, picked, precision=lax.Precision.HIGHEST)

    result = lax.map(single, (masked.reshape(TILES, KT, NB, VOX), global_id.reshape(TILES, KT, NB)))
    return result.reshape(NEURONS, 2, FH)


def spread(recon_field, trace_all, global_id):
    def single(tile_item):
        trace_tile, tile_ids = tile_item
        picked = recon_field[tile_ids].astype(jnp.float32)
        return jnp.einsum('kbpjv,kpj->kbv', picked, trace_tile, precision=lax.Precision.HIGHEST)

    result = lax.map(single, (trace_all.reshape(TILES, KT, 2, FH), global_id.reshape(TILES, KT, NB)))
    return result.reshape(NEURONS, NB, VOX)


def reference(movie, shifts, footprints, blocks, traces, counts):
    registered = register(movie, shifts)
    stacked = registered.reshape(2, Z, FH, H, W)
    stacked = jnp.pad(stacked, ((0, 0), (0, 0), (0, 0), (0, PR), (0, 0)))
    stacked = stacked.reshape(2, Z, FH, H // PR + 1, PR, XB, PC)
    field_movie = jnp.transpose(stacked, (1, 3, 5, 0, 2, 4, 6)).reshape(Z * (H // PR + 1) * XB, 2, FH, VOX)
    slot_index = jnp.arange(NEURONS, dtype=jnp.int32)
    tile_of = (slot_index // KT).astype(jnp.int32)
    alive = (slot_index % KT) < counts[tile_of]
    masked = jnp.where(alive[:, None, None], footprints, jnp.zeros_like(footprints)).astype(jnp.float32)
    global_id = global_ids(blocks, tile_of)
    old_traces = jnp.transpose(traces, (1, 0, 2))
    rebuilt = rebuild(masked, old_traces, global_id)
    numer_c = project(field_movie, masked, global_id)
    denom_c = project(rebuilt, masked, global_id) + EPSILON
    updated = old_traces * numer_c / denom_c
    rebuilt_new = rebuild(masked, updated, global_id)
    numer_a = spread(field_movie, updated, global_id)
    denom_a = spread(rebuilt_new, updated, global_id) + EPSILON
    new_footprints = (masked * numer_a / denom_a).astype(jnp.bfloat16)
    new_traces = jnp.transpose(updated, (1, 0, 2))
    return new_traces, new_footprints
```

```python
import jax
import jax.numpy as jnp
from jax import lax
from jax.experimental import pallas as pl
from jax.experimental.pallas import tpu as pltpu
from jax.sharding import PartitionSpec as P

Z = 32
PR = 8
PC = 16
VOX = PR * PC
NF = 8
KT = 96
NH = 2 * KT
NA = 4
XC = 32
FIELD = Z * XC
PADF = 4 * XC
EPSILON = 1e-06
VMEM_LIMIT = 56 * 1024 * 1024

F32 = jnp.float32
BF16 = jnp.bfloat16


def iota(shape, dim):
    return lax.broadcasted_iota(jnp.int32, shape, dim)


def vmem():
    return pl.BlockSpec(memory_space=pltpu.VMEM)


def smem():
    return pl.BlockSpec(memory_space=pltpu.SMEM)


def call(kernel, out_shape, in_specs, scratch=(), name=None):
    many = isinstance(out_shape, (list, tuple))
    return pl.pallas_call(
        kernel,
        out_shape=out_shape,
        in_specs=in_specs,
        out_specs=[vmem() for _ in out_shape] if many else vmem(),
        scratch_shapes=list(scratch),
        compiler_params=pltpu.CompilerParams(vmem_limit_bytes=VMEM_LIMIT),
        name=name,
    )


def register_kernel(shift_ref, movie_ref, out_ref):
    s = shift_ref[0]
    u = shift_ref[1]
    height, width = movie_ref.shape
    band = 128
    groups = width // 256
    src = iota((512, 256), 0) - 128
    dst = iota((512, 256), 1)
    lane = dst % 128
    column = (lane // PC) * 32 + (dst // 128) * PC + lane % PC
    pick = jnp.where(src == column - u, 1.0, 0.0).astype(BF16)
    for b in range(height // band):
        lo = max(0, b * band - 16)
        hi = min(height, b * band + band + 16)
        want = iota((band, hi - lo), 0) + b * band - s
        have = iota((band, hi - lo), 1) + lo
        move = jnp.where(want == have, 1.0, 0.0).astype(BF16)
        rows = jnp.dot(move, movie_ref[lo:hi, :], preferred_element_type=F32).astype(BF16)
        parts = []
        for g in range(groups):
            left = max(0, 256 * g - 128)
            right = min(width, 256 * g + 384)
            part = pick[left - 256 * g + 128 : right - 256 * g + 128, :]
            parts.append(jnp.dot(rows[:, left:right], part, preferred_element_type=F32))
        for t in range(band // PR):
            for c in range(2):
                piece = [p[t * PR : (t + 1) * PR, c * 128 : (c + 1) * 128] for p in parts]
                start = ((b * (band // PR) + t) * 2 + c) * groups * PR
                out_ref[start : start + groups * PR, :] = jnp.concatenate(piece, axis=0).astype(BF16)


def rows_kernel(live_ref, odd_ref, foot_ref, upper_ref, lower_ref, wide):
    wide[...] = foot_ref[...].astype(F32)
    live = live_ref[...] > 0
    odd = odd_ref[...] > 0
    for a in range(NA):
        for d, ref in ((0, upper_ref), (1, lower_ref)):
            first = wide[pl.ds(4 * a + 2 * d, KT, stride=16), :]
            second = wide[pl.ds(4 * a + 2 * d + 1, KT, stride=16), :]
            value = jnp.where(live, jnp.where(odd, second, first), 0.0)
            ref[a * KT : (a + 1) * KT, :] = value.astype(BF16)


def tile_at(ref, block):
    return ref.at[pl.ds(pl.multiple_of(block * PR, PR), PR), :]


def expand(upper_ref, lower_ref, tiles_ref):
    lane_in = iota((VOX, PR * VOX), 0)
    lane_out = iota((VOX, PR * VOX), 1)
    same = (lane_in // PC == lane_out // VOX) & (lane_in % PC == lane_out % PC)
    spread = jnp.where(same, 1.0, 0.0).astype(BF16)
    for a in range(NA):
        for d, ref in ((0, upper_ref), (1, lower_ref)):
            rows = ref[a * KT : (a + 1) * KT, :]
            wide = jnp.dot(rows, spread, preferred_element_type=F32)
            base = (a * NH + d * KT) * PR
            for i in range(PR):
                tiles_ref[pl.ds(base + i, KT, stride=PR), :] = wide[:, i * VOX : (i + 1) * VOX]


def zero(ref, rows):
    step = 256

    def body(k, carry):
        ref[pl.ds(pl.multiple_of(k * step, step), step), :] = jnp.zeros((step, VOX), F32)
        return carry

    lax.fori_loop(0, rows // step, body, 0)


def rebuild(place_ref, tiles_ref, trace_ref, field_ref):
    zero(field_ref, 2 * FIELD * PR)

    def body(n, carry):
        trace = jnp.broadcast_to(trace_ref[pl.ds(n, 1), :], (PR, VOX))
        base = place_ref[n]
        for a in range(NA):
            spot = tile_at(field_ref, base + a * XC)
            spot[...] = spot[...] + tile_at(tiles_ref, a * NH + n)[...] * trace
        return carry

    lax.fori_loop(0, NH, body, 0, unroll=4)


def project(place_ref, tiles_ref, field_ref, sums_ref):
    def body(n, carry):
        base = place_ref[n]
        total = tile_at(tiles_ref, n)[...] * tile_at(field_ref, base)[...]
        for a in range(1, NA):
            total = total + tile_at(tiles_ref, a * NH + n)[...] * tile_at(field_ref, base + a * XC)[...]
        tile_at(sums_ref, n)[...] = total
        return carry

    lax.fori_loop(0, NH, body, 0, unroll=4)
    rows = sums_ref[pl.ds(0, NH, stride=PR), :]
    for i in range(1, PR):
        rows = rows + sums_ref[pl.ds(i, NH, stride=PR), :]
    group = jnp.where(iota((VOX, VOX), 0) // PC == iota((VOX, VOX), 1) // PC, 1.0, 0.0)
    return jnp.dot(rows, group, preferred_element_type=F32, precision=lax.Precision.HIGHEST)


def denom_kernel(place_ref, upper_ref, lower_ref, trace_ref, tiles_ref, denom_ref, field, sums):
    expand(upper_ref, lower_ref, tiles_ref)
    rebuild(place_ref, tiles_ref, trace_ref, field)
    denom_ref[...] = project(place_ref, tiles_ref, field, sums)


def frames_to_lanes(tiles):
    lane = iota((PR, VOX), 1)
    for k in range(3):
        step = 1 << k
        width = PC * step
        odd = (lane // width) % 2 == 1
        after = list(tiles)
        for f in range(NF):
            if f & step:
                continue
            a, b = tiles[f], tiles[f | step]
            after[f] = jnp.where(odd, pltpu.roll(b, width, 1), a)
            after[f | step] = jnp.where(odd, b, pltpu.roll(a, VOX - width, 1))
        tiles = after
    return tiles


def numer_kernel(place_ref, tiles_ref, image_ref, field_ref, numer_ref, sums):
    def body(z, carry):
        groups = XC // 8
        rows = groups * PR
        base = pl.multiple_of(z * (NF * rows), NF * rows)
        image = image_ref[pl.ds(base, NF * rows), :].astype(F32)
        for g in range(groups):
            tiles = [image[f * rows + g * PR : f * rows + (g + 1) * PR, :] for f in range(NF)]
            tiles = frames_to_lanes(tiles)
            for x in range(8):
                tile_at(field_ref, z * XC + g * 8 + x)[...] = tiles[x]
        return carry

    lax.fori_loop(0, Z, body, 0)
    field_ref[FIELD * PR : (FIELD + PADF) * PR, :] = jnp.zeros((PADF * PR, VOX), F32)
    numer_ref[...] = project(place_ref, tiles_ref, field_ref, sums)


def fold(products_ref):
    lane_in = iota((VOX, VOX), 0)
    lane_out = iota((VOX, VOX), 1)
    total = None
    for i in range(PR):
        pick = jnp.where((lane_out // PC == i) & (lane_out % PC == lane_in % PC), 1.0, 0.0).astype(BF16)
        rows = products_ref[pl.ds(i, NA * NH, stride=PR), :]
        high = rows.astype(BF16)
        low = (rows - high.astype(F32)).astype(BF16)
        part = jnp.dot(high, pick, preferred_element_type=F32) + jnp.dot(low, pick, preferred_element_type=F32)
        total = part if total is None else total + part
    return total


def update_kernel(
    place_ref, spot_ref, upper_ref, lower_ref, tiles_ref, image_ref, old_ref, numer_ref, denom_ref,
    trace_ref, upper_out, lower_out, field, product_n, product_d,
):
    trace_ref[...] = old_ref[...] * numer_ref[...] / (denom_ref[...] + EPSILON)
    rebuild(place_ref, tiles_ref, trace_ref, field)

    def body(n, carry):
        trace = jnp.broadcast_to(trace_ref[pl.ds(n, 1), :], (PR, VOX))
        base = place_ref[n]
        spot = spot_ref[n]
        for a in range(NA):
            m = a * NH + n
            tile_at(product_n, m)[...] = tile_at(image_ref, spot + a * XC)[...] * trace
            tile_at(product_d, m)[...] = tile_at(field, base + a * XC)[...] * trace
        return carry

    lax.fori_loop(0, NH, body, 0, unroll=4)
    ratio = fold(product_n) / (fold(product_d) + EPSILON)
    for a in range(NA):
        for d, ref, out in ((0, upper_ref, upper_out), (1, lower_ref, lower_out)):
            start = a * NH + d * KT
            value = ref[a * KT : (a + 1) * KT, :].astype(F32) * ratio[start : start + KT, :]
            out[a * KT : (a + 1) * KT, :] = value.astype(BF16)


def merge_kernel(odd_ref, upper_ref, lower_ref, upper_other, lower_other, out_ref, wide):
    odd = odd_ref[...] > 0
    for a in range(NA):
        rows = slice(a * KT, (a + 1) * KT)
        for d, mine_ref, other_ref in ((0, upper_ref, upper_other), (1, lower_ref, lower_other)):
            mine = mine_ref[rows, :].astype(F32)
            other = other_ref[rows, :].astype(F32)
            wide[pl.ds(4 * a + 2 * d, KT, stride=16), :] = jnp.where(odd, other, mine)
            wide[pl.ds(4 * a + 2 * d + 1, KT, stride=16), :] = jnp.where(odd, mine, other)
    out_ref[...] = wide[...].astype(BF16)


def shards(movie, shifts, footprints, blocks, traces, counts):
    tiles = lax.axis_size("tile")
    tile = lax.axis_index("tile")
    core = lax.axis_index("nrn")
    down = [(i, (i + 1) % tiles) for i in range(tiles)]
    up = [(j, i) for i, j in down]
    cross = [(0, 1), (1, 0)]

    def shape(rows, dtype):
        return jax.ShapeDtypeStruct((rows, VOX), dtype)

    sent = call(
        register_kernel, shape(tiles * 2 * XC // 8 * PR, BF16), [smem(), vmem()], name="register"
    )(shifts[0, 0], movie[0, 0])
    images = lax.all_to_all(
        sent.reshape(tiles * 2, XC // 8 * PR, VOX), ("tile", "nrn"), split_axis=0, concat_axis=0, tiled=True
    ).reshape(-1, VOX)

    first = blocks[:, 0]
    plane = first // 128
    column = first % 64
    odd = (column + core) % 2
    base = plane * XC + (column + odd) // 2
    live = (jnp.arange(KT, dtype=jnp.int32) < counts[0]).astype(jnp.int32)
    odd_rows = jnp.broadcast_to(odd[:, None], (KT, VOX))
    live_rows = jnp.broadcast_to(live[:, None], (KT, VOX))
    upper, lower = call(
        rows_kernel, [shape(NA * KT, BF16)] * 2, [vmem()] * 3,
        scratch=[pltpu.VMEM((KT * 16, VOX), F32)], name="rows",
    )(live_rows, odd_rows, footprints.reshape(-1, VOX))

    mine = traces[0]
    theirs = lax.ppermute(mine, "nrn", cross)
    even_frames = jnp.where(core == 0, mine, theirs)
    odd_frames = jnp.where(core == 0, theirs, mine)
    frames = jnp.stack([even_frames, odd_frames], axis=-1).reshape(KT, NF)
    packet = jnp.concatenate([frames, jnp.broadcast_to(base.astype(F32)[:, None], (KT, NF))], axis=1)
    packet_in = lax.ppermute(packet, "tile", down)
    lower_in = lax.ppermute(lower, "tile", down)
    base_in = packet_in[:, NF].astype(jnp.int32)
    margin = tile == 0
    place = jnp.concatenate([base, base_in + jnp.where(margin, FIELD, 0)])
    spot = jnp.concatenate([base, jnp.where(margin, FIELD, base_in)])
    both = jnp.concatenate([frames, packet_in[:, :NF]], axis=0)
    old = jnp.broadcast_to(both[:, :, None], (NH, NF, PC)).reshape(NH, VOX)

    field = pltpu.VMEM((2 * FIELD * PR, VOX), F32)
    sums = pltpu.VMEM((NH * PR, VOX), F32)
    tiles_e, denom = call(
        denom_kernel, [shape(NA * NH * PR, F32), shape(NH, F32)], [smem()] + [vmem()] * 3,
        scratch=[field, sums], name="denominator",
    )(place, upper, lower_in, old)

    def complete(partial):
        partial = partial + lax.ppermute(partial, "nrn", cross)
        from_above = lax.ppermute(partial[:KT], "tile", down)
        from_below = lax.ppermute(partial[KT:], "tile", up)
        return partial + jnp.concatenate([from_below, from_above], axis=0)

    denom = complete(denom)
    image_field, numer = call(
        numer_kernel, [shape((FIELD + PADF) * PR, F32), shape(NH, F32)], [smem()] + [vmem()] * 2,
        scratch=[sums], name="numerator",
    )(spot, tiles_e, images)
    numer = complete(numer)

    product = pltpu.VMEM((NA * NH * PR, VOX), F32)
    new, upper_new, lower_new = call(
        update_kernel, [shape(NH, F32), shape(NA * KT, BF16), shape(NA * KT, BF16)], [smem()] * 2 + [vmem()] * 7,
        scratch=[field, product, product], name="update",
    )(place, spot, upper, lower_in, tiles_e, image_field, old, numer, denom)

    lower_back = lax.ppermute(lower_new, "tile", up)
    upper_other = lax.ppermute(upper_new, "nrn", cross)
    lower_other = lax.ppermute(lower_back, "nrn", cross)
    merged = call(
        merge_kernel, shape(KT * 16, BF16), [vmem()] * 5,
        scratch=[pltpu.VMEM((KT * 16, VOX), F32)], name="merge",
    )(odd_rows, upper_new, lower_back, upper_other, lower_other)

    frames_new = new[:KT].reshape(KT, NF, PC)[:, :, 0].reshape(KT, NF // 2, 2)
    updated = jnp.where(core == 0, frames_new[:, :, 0], frames_new[:, :, 1])
    return updated[None], merged.reshape(KT, 16, VOX)


def solution(mesh):
    placed = (
        P("nrn", "tile", None, None),
        P("nrn", "tile", None),
        P("tile", None, None),
        P("tile", None),
        P("nrn", "tile", None),
        P("tile"),
    )
    return jax.shard_map(
        shards,
        mesh=mesh,
        in_specs=placed,
        out_specs=(P("nrn", "tile", None), P("tile", None, None)),
        check_vma=False,
    )
```

```python
import jax
import jax.numpy as jnp
from jax import lax
from jax.experimental import pallas as pl
from jax.experimental.pallas import tpu as pltpu
from jax.sharding import PartitionSpec as P

Z = 32
PR = 8
PC = 16
VOX = PR * PC
BAND = 224
NF = 8
KT = 96
NH = 2 * KT
NA = 4
XC = 32
TILES = NA * NH
FIELD = Z * XC
PADF = 4 * XC
EPSILON = 1e-06
MIB = 1024 * 1024

F32 = jnp.float32
BF16 = jnp.bfloat16


def iota(shape, dim):
    return lax.broadcasted_iota(jnp.int32, shape, dim)


def vmem():
    return pl.BlockSpec(memory_space=pltpu.VMEM)


def smem():
    return pl.BlockSpec(memory_space=pltpu.SMEM)


def call(kernel, out_shape, in_specs, scratch=(), name=None, limit=24, out_specs=None):
    if out_specs is None:
        out_specs = [vmem() for _ in out_shape] if isinstance(out_shape, (list, tuple)) else vmem()
    return pl.pallas_call(
        kernel,
        out_shape=out_shape,
        in_specs=in_specs,
        out_specs=out_specs,
        scratch_shapes=list(scratch),
        compiler_params=pltpu.CompilerParams(vmem_limit_bytes=limit * MIB),
        name=name,
    )


def rows_kernel(count_ref, block_ref, foot_ref, upper_ref, packet_ref, odd_ref, wide):
    core = lax.axis_index("nrn")
    first = block_ref[...]
    ones = jnp.where(iota((16, VOX), 0) == 0, 1.0, 0.0).astype(BF16)

    def down_rows(values):
        return lax.dot_general(
            values.astype(F32).astype(BF16), ones, (((0,), (0,)), ((), ())), preferred_element_type=F32
        )

    plane = down_rows(first // 128)
    column = down_rows(first % 64).astype(jnp.int32)
    odd = (column + core) % 2
    place = (column + odd) // 2
    live = iota((KT, VOX), 0) < count_ref[0]
    odd_ref[...] = odd
    info = jnp.where(iota((KT, VOX), 1) < 64, plane, place.astype(F32))
    packet_ref[NA * KT : NA * KT + KT, :] = info.astype(BF16)
    wide[...] = foot_ref[...].astype(F32)
    for a in range(NA):
        for d, ref in ((0, upper_ref), (1, packet_ref)):
            left = wide[pl.ds(4 * a + 2 * d, KT, stride=16), :]
            right = wide[pl.ds(4 * a + 2 * d + 1, KT, stride=16), :]
            value = jnp.where(live, jnp.where(odd > 0, right, left), 0.0)
            ref[a * KT : (a + 1) * KT, :] = value.astype(BF16)


def register_kernel(shift_ref, movie_ref, out_ref, image, laid, load_sem, store_sem):
    height, width = movie_ref.shape
    bands = [(lo, min(height, lo + BAND)) for lo in range(0, height, BAND)]
    edges = [0] + [min(height, hi + 16) for _, hi in bands]
    loads = []
    for b in range(len(bands)):
        rows = pl.ds(edges[b], edges[b + 1] - edges[b])
        loads.append(pltpu.make_async_copy(movie_ref.at[rows, :], image.at[rows, :], load_sem.at[b]))
        loads[-1].start()
    s = shift_ref[0]
    u = shift_ref[1]
    groups = width // 256
    src = iota((512, 256), 0) - 128
    lane = iota((512, 256), 1) % 128
    want_column = (lane // PC) * 32 + (iota((512, 256), 1) // 128) * PC + lane % PC
    pick = jnp.where(src == want_column - u, 1.0, 0.0).astype(BF16)
    stores = []
    for b, (first, last) in enumerate(bands):
        loads[b].wait()
        lo = max(0, first - 16)
        hi = min(height, last + 16)
        want = iota((last - first, hi - lo), 0) + first - s
        have = iota((last - first, hi - lo), 1) + lo
        move = jnp.where(want == have, 1.0, 0.0).astype(BF16)
        rows = jnp.dot(move, image[lo:hi, :], preferred_element_type=F32).astype(BF16)
        parts = []
        for g in range(groups):
            start = max(0, 256 * g - 128)
            stop = min(width, 256 * g + 384)
            part = pick[start - 256 * g + 128 : stop - 256 * g + 128, :]
            parts.append(jnp.dot(rows[:, start:stop], part, preferred_element_type=F32))
        for t in range((last - first) // PR):
            for c in range(2):
                piece = [p[t * PR : (t + 1) * PR, c * 128 : (c + 1) * 128] for p in parts]
                at = ((first // PR + t) * 2 + c) * groups * PR
                laid[at : at + groups * PR, :] = jnp.concatenate(piece, axis=0).astype(BF16)
        where = pl.ds(first * 2 * groups, (last - first) * 2 * groups)
        stores.append(pltpu.make_async_copy(laid.at[where, :], out_ref.at[where, :], store_sem.at[b]))
        stores[-1].start()
    for copy in stores:
        copy.wait()


def tile_at(ref, block):
    return ref.at[pl.ds(pl.multiple_of(block * PR, PR), PR), :]


def expand(upper_ref, lower_ref, tiles_ref):
    lane_in = iota((VOX, PR * VOX), 0)
    lane_out = iota((VOX, PR * VOX), 1)
    same = (lane_in // PC == lane_out // VOX) & (lane_in % PC == lane_out % PC)
    spread = jnp.where(same, 1.0, 0.0).astype(BF16)
    for a in range(NA):
        for d, ref in ((0, upper_ref), (1, lower_ref)):
            rows = ref[a * KT : (a + 1) * KT, :]
            wide = jnp.dot(rows, spread, preferred_element_type=F32)
            base = (a * NH + d * KT) * PR
            for i in range(PR):
                tiles_ref[pl.ds(base + i, KT, stride=PR), :] = wide[:, i * VOX : (i + 1) * VOX]


def zero(ref, start, rows):
    step = 256

    def body(k, carry):
        ref[pl.ds(pl.multiple_of(start + k * step, step), step), :] = jnp.zeros((step, VOX), F32)
        return carry

    lax.fori_loop(0, rows // step, body, 0)


def rebuild(place_ref, tiles_ref, trace_ref, field_ref):
    zero(field_ref, 0, FIELD * PR)

    @pl.when(lax.axis_index("tile") == 0)
    def _():
        zero(field_ref, FIELD * PR, FIELD * PR)

    def body(n, carry):
        trace = jnp.broadcast_to(trace_ref[pl.ds(n, 1), :], (PR, VOX))
        base = place_ref[n]
        held = [tile_at(field_ref, base + a * XC)[...] for a in range(NA)]
        added = [tile_at(tiles_ref, a * NH + n)[...] * trace for a in range(NA)]
        for a in range(NA):
            tile_at(field_ref, base + a * XC)[...] = held[a] + added[a]
        return carry

    lax.fori_loop(0, NH, body, 0, unroll=8)


def project(place_ref, tiles_ref, field_ref, sums_ref):
    def body(n, carry):
        base = place_ref[n]
        total = tile_at(tiles_ref, n)[...] * tile_at(field_ref, base)[...]
        for a in range(1, NA):
            total = total + tile_at(tiles_ref, a * NH + n)[...] * tile_at(field_ref, base + a * XC)[...]
        tile_at(sums_ref, n)[...] = total
        return carry

    lax.fori_loop(0, NH, body, 0, unroll=8)
    rows = sums_ref[pl.ds(0, NH, stride=PR), :]
    for i in range(1, PR):
        rows = rows + sums_ref[pl.ds(i, NH, stride=PR), :]
    group = jnp.where(iota((VOX, VOX), 0) // PC == iota((VOX, VOX), 1) // PC, 1.0, 0.0)
    return jnp.dot(rows, group, preferred_element_type=F32, precision=lax.Precision.HIGHEST)


def denom_kernel(place_ref, upper_ref, packet_ref, trace_ref, tiles_ref, field, sums):
    expand(upper_ref, packet_ref, tiles_ref)
    rebuild(place_ref, tiles_ref, trace_ref, field)
    tiles_ref[TILES * PR : TILES * PR + NH, :] = project(place_ref, tiles_ref, field, sums)


def numer_kernel(place_ref, tiles_ref, image_ref, field_ref, sums_ref, permute_ref, sums):
    source = iota((VOX, NF * VOX), 0)
    target = iota((VOX, NF * VOX), 1)
    same = (source // PC == target // VOX) & (source % PC == target % PC)
    frame = (target % VOX) // PC
    for f in range(NF):
        permute_ref[f * VOX : (f + 1) * VOX, :] = jnp.where(same & (frame == f), 1.0, 0.0).astype(BF16)
    groups = XC // 8
    rows = groups * PR
    step = 16

    def body(k, carry):
        base = pl.multiple_of(k * (step * NF * rows), step * NF * rows)
        image = image_ref[pl.ds(base, step * NF * rows), :]
        lhs = []
        for z in range(step):
            start = z * NF * rows
            lhs.append(jnp.concatenate([image[start + f * rows : start + (f + 1) * rows, :] for f in range(NF)], axis=1))
        out = jnp.dot(jnp.concatenate(lhs, axis=0), permute_ref[...], preferred_element_type=F32)
        for z in range(step):
            for g in range(groups):
                for x in range(8):
                    at = z * rows + g * PR
                    tile_at(field_ref, (k * step + z) * XC + g * 8 + x)[...] = out[at : at + PR, x * VOX : (x + 1) * VOX]
        return carry

    lax.fori_loop(0, Z // step, body, 0)
    field_ref[FIELD * PR : (FIELD + PADF) * PR, :] = jnp.zeros((PADF * PR, VOX), F32)
    numer = project(place_ref, tiles_ref, field_ref, sums)
    denom = tiles_ref[TILES * PR : TILES * PR + NH, :]
    value = jnp.where(iota((NH, VOX), 1) % PC < PC // 2, numer, denom)
    sums_ref[...] = value


def fold(products_ref):
    lane_in = iota((2 * VOX, VOX), 0) % VOX
    lane_out = iota((2 * VOX, VOX), 1)
    total = None
    for i in range(PR):
        pick = jnp.where((lane_out // PC == i) & (lane_out % PC == lane_in % PC), 1.0, 0.0).astype(BF16)
        rows = products_ref[pl.ds(i, NA * KT, stride=PR), :]
        high = rows.astype(BF16)
        low = (rows - high.astype(F32)).astype(BF16)
        part = jnp.dot(jnp.concatenate([high, low], axis=1), pick, preferred_element_type=F32)
        total = part if total is None else total + part
    return total


def renew(start, place_ref, spot_ref, rows_ref, image_ref, field_ref, trace_ref, product_n, product_d):
    def body(k, carry):
        n = start + k
        trace = jnp.broadcast_to(trace_ref[pl.ds(n, 1), :], (PR, VOX))
        base = place_ref[n]
        spot = spot_ref[n]
        for a in range(NA):
            m = a * KT + k
            tile_at(product_n, m)[...] = tile_at(image_ref, spot + a * XC)[...] * trace
            tile_at(product_d, m)[...] = tile_at(field_ref, base + a * XC)[...] * trace
        return carry

    lax.fori_loop(0, KT, body, 0, unroll=8)
    ratio = fold(product_n) / (fold(product_d) + EPSILON)
    return (rows_ref[0 : NA * KT, :].astype(F32) * ratio).astype(BF16)


def lower_kernel(
    place_ref, spot_ref, packet_ref, tiles_ref, image_ref, old_ref, mine_ref, below_ref, above_ref,
    trace_ref, field_ref, out_ref, product_n, product_d,
):
    sums = mine_ref[...] + jnp.concatenate([below_ref[...], above_ref[...]], axis=0)
    first = iota((NH, VOX), 1) % PC < PC // 2
    numer = jnp.where(first, sums, pltpu.roll(sums, PC // 2, 1))
    denom = jnp.where(first, pltpu.roll(sums, VOX - PC // 2, 1), sums)
    trace_ref[...] = old_ref[...] * numer / (denom + EPSILON)
    rebuild(place_ref, tiles_ref, trace_ref, field_ref)
    out_ref[...] = renew(
        KT, place_ref, spot_ref, packet_ref, image_ref, field_ref, trace_ref, product_n, product_d
    )


def upper_kernel(
    place_ref, spot_ref, upper_ref, image_ref, field_ref, trace_ref, out_ref, sent_ref, product_n, product_d
):
    value = renew(0, place_ref, spot_ref, upper_ref, image_ref, field_ref, trace_ref, product_n, product_d)
    out_ref[...] = value
    sent_ref[...] = value


def merge_kernel(odd_ref, upper_ref, lower_ref, upper_other, lower_other, out_ref, wide):
    odd = odd_ref[...] > 0
    for a in range(NA):
        rows = slice(a * KT, (a + 1) * KT)
        for d, mine_ref, other_ref in ((0, upper_ref, upper_other), (1, lower_ref, lower_other)):
            mine = mine_ref[rows, :].astype(F32)
            other = other_ref[rows, :].astype(F32)
            wide[pl.ds(4 * a + 2 * d, KT, stride=16), :] = jnp.where(odd, other, mine)
            wide[pl.ds(4 * a + 2 * d + 1, KT, stride=16), :] = jnp.where(odd, mine, other)
    out_ref[...] = wide[...].astype(BF16)


def shards(movie, shifts, footprints, blocks, traces, counts):
    tiles = lax.axis_size("tile")
    tile = lax.axis_index("tile")
    core = lax.axis_index("nrn")
    down = [(i, (i + 1) % tiles) for i in range(tiles)]
    up = [(j, i) for i, j in down]
    cross = [(0, 1), (1, 0)]

    def shape(rows, dtype):
        return jax.ShapeDtypeStruct((rows, VOX), dtype)

    mine = traces[0]
    above = lax.ppermute(mine, "tile", down)
    theirs = lax.ppermute(mine, "nrn", cross)

    upper, packet, odd = call(
        rows_kernel,
        [shape(NA * KT, BF16), shape(NA * KT + KT, BF16), shape(KT, jnp.int32)],
        [smem(), vmem(), vmem()],
        scratch=[pltpu.VMEM((KT * 16, VOX), F32)], name="rows", limit=4,
    )(
        counts, pltpu.with_memory_space_constraint(blocks.T, pltpu.HBM),
        pltpu.with_memory_space_constraint(footprints.reshape(-1, VOX), pltpu.HBM),
    )
    packet_in = lax.ppermute(packet, "tile", down)

    height, width = movie.shape[2:]
    outside = pl.BlockSpec(memory_space=pltpu.HBM)
    sent = call(
        register_kernel, shape(tiles * 2 * XC, BF16), [smem(), outside],
        scratch=[
            pltpu.VMEM((height, width), BF16), pltpu.VMEM((tiles * 2 * XC, VOX), BF16),
            pltpu.SemaphoreType.DMA((5,)), pltpu.SemaphoreType.DMA((5,)),
        ],
        out_specs=outside, name="register", limit=12,
    )(shifts[0, 0], pltpu.with_memory_space_constraint(movie[0, 0], pltpu.HBM))
    sent, packet_in, above, theirs = lax.optimization_barrier((sent, packet_in, above, theirs))
    images = lax.all_to_all(
        sent.reshape(tiles * 2, XC, VOX), ("tile", "nrn"), split_axis=0, concat_axis=0, tiled=True
    ).reshape(-1, VOX)

    both = jnp.concatenate([mine, above], axis=0)
    other = jnp.concatenate([theirs, lax.ppermute(above, "nrn", cross)], axis=0)
    frames = jnp.stack([jnp.where(core == 0, both, other), jnp.where(core == 0, other, both)], axis=-1)
    old = jnp.broadcast_to(frames.reshape(NH, NF)[:, :, None], (NH, NF, PC)).reshape(NH, VOX)

    def base_of(info):
        return info[NA * KT :, 0].astype(jnp.int32) * XC + info[NA * KT :, 64].astype(jnp.int32)

    base, base_in = base_of(packet), base_of(packet_in)
    margin = tile == 0
    place = jnp.concatenate([base, base_in + jnp.where(margin, FIELD, 0)])
    spot = jnp.concatenate([base, jnp.where(margin, FIELD, base_in)])

    field = pltpu.VMEM((2 * FIELD * PR, VOX), F32)
    sums = pltpu.VMEM((NH * PR, VOX), F32)
    in_vmem = pltpu.with_memory_space_constraint
    tiles_e = call(
        denom_kernel, pltpu.VMEM((TILES * PR + NH, VOX), F32), [smem()] + [vmem()] * 3,
        scratch=[field, sums], name="denominator", limit=14,
    )(place, upper, packet_in, old)
    tiles_e = in_vmem(tiles_e, pltpu.VMEM)
    image_field, partial = call(
        numer_kernel, [pltpu.VMEM(((FIELD + PADF) * PR, VOX), F32), shape(NH, F32)],
        [smem()] + [vmem()] * 2,
        scratch=[pltpu.VMEM((NF * VOX, NF * VOX), BF16), sums], name="numerator", limit=12,
    )(spot, tiles_e, images)
    image_field = in_vmem(image_field, pltpu.VMEM)

    everyone = ("tile", "nrn")

    def other_core(pairs):
        return [(2 * i + c, 2 * j + 1 - c) for i, j in pairs for c in (0, 1)]

    partial = partial + lax.ppermute(partial, "nrn", cross)
    from_above = lax.ppermute(partial[:KT], "tile", down)
    from_below = lax.ppermute(partial[KT:], "tile", up)

    product = pltpu.VMEM((NA * KT * PR, VOX), F32)
    new, rebuilt, lower_new = call(
        lower_kernel,
        [shape(NH, F32), pltpu.VMEM((2 * FIELD * PR, VOX), F32), shape(NA * KT, BF16)],
        [smem()] * 2 + [vmem()] * 7,
        scratch=[product, product], name="lower", limit=8,
    )(place, spot, packet_in, tiles_e, image_field, old, partial, from_below, from_above)
    lower_back = lax.ppermute(lower_new, "tile", up)
    lower_other = lax.ppermute(lower_new, everyone, other_core(up))
    upper_new, upper_sent = call(
        upper_kernel, [shape(NA * KT, BF16)] * 2, [smem()] * 2 + [vmem()] * 4,
        scratch=[product, product], name="upper", limit=8,
    )(place, spot, upper, image_field, in_vmem(rebuilt, pltpu.VMEM), new)
    upper_other = lax.ppermute(upper_sent, "nrn", cross)
    merged = call(
        merge_kernel, shape(KT * 16, BF16), [vmem()] * 5,
        scratch=[pltpu.VMEM((KT * 16, VOX), F32)], name="merge", limit=4,
    )(odd, upper_new, lower_back, upper_other, lower_other)

    frames_new = new[:KT].reshape(KT, NF, PC)[:, :, 0].reshape(KT, NF // 2, 2)
    updated = jnp.where(core == 0, frames_new[:, :, 0], frames_new[:, :, 1])
    return updated[None], merged.reshape(KT, 16, VOX)


def solution(mesh):
    placed = (
        P("nrn", "tile", None, None),
        P("nrn", "tile", None),
        P("tile", None, None),
        P("tile", None),
        P("nrn", "tile", None),
        P("tile"),
    )
    return jax.shard_map(
        shards,
        mesh=mesh,
        in_specs=placed,
        out_specs=(P("nrn", "tile", None), P("tile", None, None)),
        check_vma=False,
    )
```

```python
import jax
import jax.numpy as jnp
from jax import lax
from jax.experimental import pallas as pl
from jax.experimental.pallas import tpu as pltpu
from jax.sharding import PartitionSpec as P

Z = 32
PR = 8
PC = 16
VOX = PR * PC
BAND = 224
NF = 8
KT = 96
NH = 2 * KT
NA = 4
XC = 32
TILES = NA * NH
FIELD = Z * XC
PADF = 4 * XC
EPSILON = 1e-06
MIB = 1024 * 1024

F32 = jnp.float32
BF16 = jnp.bfloat16


def iota(shape, dim):
    return lax.broadcasted_iota(jnp.int32, shape, dim)


def vmem():
    return pl.BlockSpec(memory_space=pltpu.VMEM)


def smem():
    return pl.BlockSpec(memory_space=pltpu.SMEM)


def call(kernel, out_shape, in_specs, scratch=(), name=None, limit=24, out_specs=None):
    if out_specs is None:
        out_specs = [vmem() for _ in out_shape] if isinstance(out_shape, (list, tuple)) else vmem()
    return pl.pallas_call(
        kernel,
        out_shape=out_shape,
        in_specs=in_specs,
        out_specs=out_specs,
        scratch_shapes=list(scratch),
        compiler_params=pltpu.CompilerParams(vmem_limit_bytes=limit * MIB),
        name=name,
    )


def places(block_ref):
    first = block_ref[...]
    ones = jnp.where(iota((16, VOX), 0) == 0, 1.0, 0.0).astype(BF16)

    def down_rows(values):
        return lax.dot_general(
            values.astype(F32).astype(BF16), ones, (((0,), (0,)), ((), ())), preferred_element_type=F32
        )

    plane = down_rows(first // 128)
    column = down_rows(first % 64).astype(jnp.int32)
    odd = (column + lax.axis_index("nrn")) % 2
    return plane, (column + odd) // 2, odd


def pick_rows(d, count_ref, odd, foot_ref, out_ref, wide):
    wide[...] = foot_ref[...].astype(F32)
    live = iota((KT, VOX), 0) < count_ref[0]
    for a in range(NA):
        left = wide[pl.ds(4 * a + 2 * d, KT, stride=16), :]
        right = wide[pl.ds(4 * a + 2 * d + 1, KT, stride=16), :]
        value = jnp.where(live, jnp.where(odd > 0, right, left), 0.0)
        out_ref[a * KT : (a + 1) * KT, :] = value.astype(BF16)


def rows_kernel(count_ref, block_ref, foot_ref, packet_ref, upper_ref, odd_ref, wide):
    plane, place, odd = places(block_ref)
    info = jnp.where(iota((KT, VOX), 1) < 64, plane, place.astype(F32))
    packet_ref[NA * KT : NA * KT + KT, :] = info.astype(BF16)
    pick_rows(1, count_ref, odd, foot_ref, packet_ref, wide)
    odd_ref[...] = odd
    pick_rows(0, count_ref, odd, foot_ref, upper_ref, wide)


def register_kernel(shift_ref, movie_ref, out_ref, image, laid, load_sem, store_sem):
    height, width = movie_ref.shape
    bands = [(lo, min(height, lo + BAND)) for lo in range(0, height, BAND)]
    edges = [0] + [min(height, hi + 16) for _, hi in bands]
    loads = []
    for b in range(len(bands)):
        rows = pl.ds(edges[b], edges[b + 1] - edges[b])
        loads.append(pltpu.make_async_copy(movie_ref.at[rows, :], image.at[rows, :], load_sem.at[b]))
        loads[-1].start()
    s = shift_ref[0]
    u = shift_ref[1]
    groups = width // 256
    src = iota((512, 256), 0) - 128
    lane = iota((512, 256), 1) % 128
    want_column = (lane // PC) * 32 + (iota((512, 256), 1) // 128) * PC + lane % PC
    pick = jnp.where(src == want_column - u, 1.0, 0.0).astype(BF16)
    stores = []
    for b, (first, last) in enumerate(bands):
        loads[b].wait()
        lo = max(0, first - 16)
        hi = min(height, last + 16)
        want = iota((last - first, hi - lo), 0) + first - s
        have = iota((last - first, hi - lo), 1) + lo
        move = jnp.where(want == have, 1.0, 0.0).astype(BF16)
        rows = jnp.dot(move, image[lo:hi, :], preferred_element_type=F32).astype(BF16)
        parts = []
        for g in range(groups):
            start = max(0, 256 * g - 128)
            stop = min(width, 256 * g + 384)
            part = pick[start - 256 * g + 128 : stop - 256 * g + 128, :]
            parts.append(jnp.dot(rows[:, start:stop], part, preferred_element_type=F32))
        for t in range((last - first) // PR):
            for c in range(2):
                piece = [p[t * PR : (t + 1) * PR, c * 128 : (c + 1) * 128] for p in parts]
                at = ((first // PR + t) * 2 + c) * groups * PR
                laid[at : at + groups * PR, :] = jnp.concatenate(piece, axis=0).astype(BF16)
        where = pl.ds(first * 2 * groups, (last - first) * 2 * groups)
        stores.append(pltpu.make_async_copy(laid.at[where, :], out_ref.at[where, :], store_sem.at[b]))
        stores[-1].start()
    for copy in stores:
        copy.wait()


def tile_at(ref, block):
    return ref.at[pl.ds(pl.multiple_of(block * PR, PR), PR), :]


def expand(upper_ref, lower_ref, tiles_ref):
    lane_in = iota((VOX, PR * VOX), 0)
    lane_out = iota((VOX, PR * VOX), 1)
    same = (lane_in // PC == lane_out // VOX) & (lane_in % PC == lane_out % PC)
    spread = jnp.where(same, 1.0, 0.0).astype(BF16)
    for a in range(NA):
        for d, ref in ((0, upper_ref), (1, lower_ref)):
            rows = ref[a * KT : (a + 1) * KT, :]
            wide = jnp.dot(rows, spread, preferred_element_type=F32)
            base = (a * NH + d * KT) * PR
            for i in range(PR):
                tiles_ref[pl.ds(base + i, KT, stride=PR), :] = wide[:, i * VOX : (i + 1) * VOX]


def zero(ref, start, rows):
    step = 256

    def body(k, carry):
        ref[pl.ds(pl.multiple_of(start + k * step, step), step), :] = jnp.zeros((step, VOX), F32)
        return carry

    lax.fori_loop(0, rows // step, body, 0)


def rebuild(place_ref, tiles_ref, trace_ref, field_ref):
    zero(field_ref, 0, FIELD * PR)

    @pl.when(lax.axis_index("tile") == 0)
    def _():
        zero(field_ref, FIELD * PR, FIELD * PR)

    def body(n, carry):
        trace = jnp.broadcast_to(trace_ref[pl.ds(n, 1), :], (PR, VOX))
        base = place_ref[n]
        held = [tile_at(field_ref, base + a * XC)[...] for a in range(NA)]
        added = [tile_at(tiles_ref, a * NH + n)[...] * trace for a in range(NA)]
        for a in range(NA):
            tile_at(field_ref, base + a * XC)[...] = held[a] + added[a]
        return carry

    lax.fori_loop(0, NH, body, 0, unroll=8)


def project(place_ref, tiles_ref, field_ref, sums_ref):
    def body(n, carry):
        base = place_ref[n]
        total = tile_at(tiles_ref, n)[...] * tile_at(field_ref, base)[...]
        for a in range(1, NA):
            total = total + tile_at(tiles_ref, a * NH + n)[...] * tile_at(field_ref, base + a * XC)[...]
        tile_at(sums_ref, n)[...] = total
        return carry

    lax.fori_loop(0, NH, body, 0, unroll=8)
    rows = sums_ref[pl.ds(0, NH, stride=PR), :]
    for i in range(1, PR):
        rows = rows + sums_ref[pl.ds(i, NH, stride=PR), :]
    group = jnp.where(iota((VOX, VOX), 0) // PC == iota((VOX, VOX), 1) // PC, 1.0, 0.0)
    return jnp.dot(rows, group, preferred_element_type=F32, precision=lax.Precision.HIGHEST)


def denom_kernel(
    place_ref, upper_ref, packet_ref, trace_ref, tiles_ref, field, sums
):
    expand(upper_ref, packet_ref, tiles_ref)
    rebuild(place_ref, tiles_ref, trace_ref, field)
    tiles_ref[TILES * PR : TILES * PR + NH, :] = project(place_ref, tiles_ref, field, sums)


def even_tile():
    return lax.bitwise_and(lax.axis_index("tile"), 1) == 0


def numer_kernel(place_ref, tiles_ref, image_ref, field_ref, sums_ref, permute_ref, sums):
    source = iota((VOX, NF * VOX), 0)
    target = iota((VOX, NF * VOX), 1)
    same = (source // PC == target // VOX) & (source % PC == target % PC)
    same = jnp.where(same, 1.0, 0.0).astype(BF16)
    frame = iota((16, NF * VOX), 1) % VOX // PC
    for f in range(NF):
        mine = jnp.where(frame == f, 1.0, 0.0).astype(BF16)
        for r in range(VOX // 16):
            at = f * VOX + 16 * r
            permute_ref[at : at + 16, :] = same[16 * r : 16 * r + 16, :] * mine
    groups = XC // 8
    rows = groups * PR
    step = 16

    def body(k, carry):
        base = pl.multiple_of(k * (step * NF * rows), step * NF * rows)
        image = image_ref[pl.ds(base, step * NF * rows), :]
        lhs = []
        for z in range(step):
            start = z * NF * rows
            lhs.append(jnp.concatenate([image[start + f * rows : start + (f + 1) * rows, :] for f in range(NF)], axis=1))
        out = jnp.dot(jnp.concatenate(lhs, axis=0), permute_ref[...], preferred_element_type=F32)
        for z in range(step):
            for g in range(groups):
                for x in range(8):
                    at = z * rows + g * PR
                    tile_at(field_ref, (k * step + z) * XC + g * 8 + x)[...] = out[at : at + PR, x * VOX : (x + 1) * VOX]
        return carry

    lax.fori_loop(0, Z // step, body, 0)
    field_ref[FIELD * PR : (FIELD + PADF) * PR, :] = jnp.zeros((PADF * PR, VOX), F32)
    numer = project(place_ref, tiles_ref, field_ref, sums)
    denom = tiles_ref[TILES * PR : TILES * PR + NH, :]
    value = jnp.where(iota((NH, VOX), 1) % PC < PC // 2, numer, denom)
    upper, lower = value[:KT, :], value[KT:, :]
    even = even_tile()
    sums_ref[:KT, :] = jnp.where(even, lower, upper)
    sums_ref[KT:, :] = jnp.where(even, upper, lower)


def fold(products_ref):
    lane_in = iota((2 * VOX, VOX), 0) % VOX
    lane_out = iota((2 * VOX, VOX), 1)
    total = None
    for i in range(PR):
        pick = jnp.where((lane_out // PC == i) & (lane_out % PC == lane_in % PC), 1.0, 0.0).astype(BF16)
        rows = products_ref[pl.ds(i, NA * KT, stride=PR), :]
        high = rows.astype(BF16)
        low = (rows - high.astype(F32)).astype(BF16)
        part = jnp.dot(jnp.concatenate([high, low], axis=1), pick, preferred_element_type=F32)
        total = part if total is None else total + part
    return total


def renew(start, place_ref, spot_ref, rows_ref, image_ref, field_ref, trace_ref, product_n, product_d):
    def body(k, carry):
        n = start + k
        trace = jnp.broadcast_to(trace_ref[pl.ds(n, 1), :], (PR, VOX))
        base = place_ref[n]
        spot = spot_ref[n]
        for a in range(NA):
            m = a * KT + k
            tile_at(product_n, m)[...] = tile_at(image_ref, spot + a * XC)[...] * trace
            tile_at(product_d, m)[...] = tile_at(field_ref, base + a * XC)[...] * trace
        return carry

    lax.fori_loop(0, KT, body, 0, unroll=8)
    ratio = fold(product_n) / (fold(product_d) + EPSILON)
    return (rows_ref[0 : NA * KT, :].astype(F32) * ratio).astype(BF16)


def lower_kernel(
    place_ref, spot_ref, packet_ref, tiles_ref, image_ref, old_ref, mine_ref, near_ref, far_ref,
    trace_ref, field_ref, out_ref, product_n, product_d,
):
    even = even_tile()
    first_mine, second_mine = mine_ref[:KT, :], mine_ref[KT:, :]
    near, far = near_ref[...], far_ref[...]
    upper = jnp.where(even, second_mine + near, first_mine + far)
    lower = jnp.where(even, first_mine + far, second_mine + near)
    sums = jnp.concatenate([upper, lower], axis=0)
    first = iota((NH, VOX), 1) % PC < PC // 2
    numer = jnp.where(first, sums, pltpu.roll(sums, PC // 2, 1))
    denom = jnp.where(first, pltpu.roll(sums, VOX - PC // 2, 1), sums)
    trace_ref[...] = old_ref[...] * numer / (denom + EPSILON)
    rebuild(place_ref, tiles_ref, trace_ref, field_ref)
    out_ref[...] = renew(
        KT, place_ref, spot_ref, packet_ref, image_ref, field_ref, trace_ref, product_n, product_d
    )


def upper_kernel(
    place_ref, spot_ref, upper_ref, image_ref, field_ref, trace_ref, out_ref, sent_ref, product_n, product_d
):
    value = renew(0, place_ref, spot_ref, upper_ref, image_ref, field_ref, trace_ref, product_n, product_d)
    out_ref[...] = value
    sent_ref[...] = value


def merge_kernel(odd_ref, upper_ref, lower_ref, upper_other, lower_other, out_ref, wide):
    odd = odd_ref[...] > 0
    for a in range(NA):
        rows = slice(a * KT, (a + 1) * KT)
        for d, mine_ref, other_ref in ((0, upper_ref, upper_other), (1, lower_ref, lower_other)):
            mine = mine_ref[rows, :].astype(F32)
            other = other_ref[rows, :].astype(F32)
            wide[pl.ds(4 * a + 2 * d, KT, stride=16), :] = jnp.where(odd, other, mine)
            wide[pl.ds(4 * a + 2 * d + 1, KT, stride=16), :] = jnp.where(odd, mine, other)
    out_ref[...] = wide[...].astype(BF16)


def shards(movie, shifts, footprints, blocks, traces, counts):
    tiles = lax.axis_size("tile")
    tile = lax.axis_index("tile")
    core = lax.axis_index("nrn")
    down = [(i, (i + 1) % tiles) for i in range(tiles)]
    up = [(j, i) for i, j in down]
    cross = [(0, 1), (1, 0)]

    def shape(rows, dtype):
        return jax.ShapeDtypeStruct((rows, VOX), dtype)

    mine = traces[0]
    above = lax.ppermute(mine, "tile", down)
    theirs = lax.ppermute(mine, "nrn", cross)

    hbm = pltpu.with_memory_space_constraint
    block_rows = hbm(blocks.T, pltpu.HBM)
    foot_rows = hbm(footprints.reshape(-1, VOX), pltpu.HBM)
    wide = pltpu.VMEM((KT * 16, VOX), F32)
    packet, upper, odd = call(
        rows_kernel, [shape(NA * KT + KT, BF16), pltpu.HBM((NA * KT, VOX), BF16), shape(KT, jnp.int32)], [smem(), vmem(), vmem()], scratch=[wide], name="rows", limit=4,
    )(counts, block_rows, foot_rows)
    packet_in = lax.ppermute(packet, "tile", down)

    height, width = movie.shape[2:]
    outside = pl.BlockSpec(memory_space=pltpu.HBM)
    sent = call(
        register_kernel, shape(tiles * 2 * XC, BF16), [smem(), outside],
        scratch=[
            pltpu.VMEM((height, width), BF16), pltpu.VMEM((tiles * 2 * XC, VOX), BF16),
            pltpu.SemaphoreType.DMA((5,)), pltpu.SemaphoreType.DMA((5,)),
        ],
        out_specs=outside, name="register", limit=12,
    )(hbm(shifts[0, 0], pltpu.HBM), hbm(movie[0, 0], pltpu.HBM))
    sent, packet_in, above, theirs = lax.optimization_barrier((sent, packet_in, above, theirs))
    images = lax.all_to_all(
        sent.reshape(tiles * 2, XC, VOX), ("tile", "nrn"), split_axis=0, concat_axis=0, tiled=True
    ).reshape(-1, VOX)

    both = jnp.concatenate([mine, above], axis=0)
    other = jnp.concatenate([theirs, lax.ppermute(above, "nrn", cross)], axis=0)
    frames = jnp.stack([jnp.where(core == 0, both, other), jnp.where(core == 0, other, both)], axis=-1)
    old = jnp.broadcast_to(frames.reshape(NH, NF)[:, :, None], (NH, NF, PC)).reshape(NH, VOX)

    def base_of(info):
        return info[NA * KT :, 0].astype(jnp.int32) * XC + info[NA * KT :, 64].astype(jnp.int32)

    base, base_in = base_of(packet), base_of(packet_in)
    margin = tile == 0
    place = jnp.concatenate([base, base_in + jnp.where(margin, FIELD, 0)])
    spot = jnp.concatenate([base, jnp.where(margin, FIELD, base_in)])

    field = pltpu.VMEM((2 * FIELD * PR, VOX), F32)
    sums = pltpu.VMEM((NH * PR, VOX), F32)
    in_vmem = pltpu.with_memory_space_constraint
    tiles_e = call(
        denom_kernel, pltpu.VMEM((TILES * PR + NH, VOX), F32), [smem()] + [vmem()] * 3,
        scratch=[field, sums], name="denominator", limit=14,
    )(place, upper, packet_in, old)
    tiles_e = in_vmem(tiles_e, pltpu.VMEM)
    image_field, partial = call(
        numer_kernel, [pltpu.VMEM(((FIELD + PADF) * PR, VOX), F32), shape(NH, F32)],
        [smem()] + [vmem()] * 2,
        scratch=[pltpu.VMEM((NF * VOX, NF * VOX), BF16), sums], name="numerator", limit=12,
    )(spot, tiles_e, images)
    image_field = in_vmem(image_field, pltpu.VMEM)

    everyone = ("tile", "nrn")

    def other_core(pairs):
        return [(2 * i + c, 2 * j + 1 - c) for i, j in pairs for c in (0, 1)]

    partial = partial + lax.ppermute(partial, "nrn", cross)
    near = [(i, i ^ 1) for i in range(tiles)]
    far = [(i, (i - 1 + 2 * (i % 2)) % tiles) for i in range(tiles)]
    from_far = lax.ppermute(partial[:KT], "tile", far)
    from_near = lax.ppermute(partial[KT:], "tile", near)

    product = pltpu.VMEM((NA * KT * PR, VOX), F32)
    new, rebuilt, lower_new = call(
        lower_kernel,
        [shape(NH, F32), pltpu.VMEM((2 * FIELD * PR, VOX), F32), shape(NA * KT, BF16)],
        [smem()] * 2 + [vmem()] * 7,
        scratch=[product, product], name="lower", limit=8,
    )(place, spot, packet_in, tiles_e, image_field, old, partial, from_near, from_far)
    lower_back = lax.ppermute(lower_new, "tile", up)
    lower_other = lax.ppermute(lower_new, everyone, other_core(up))
    upper_new, upper_sent = call(
        upper_kernel, [shape(NA * KT, BF16)] * 2, [smem()] * 2 + [vmem()] * 4,
        scratch=[product, product], name="upper", limit=8,
    )(place, spot, upper, image_field, in_vmem(rebuilt, pltpu.VMEM), new)
    upper_other = lax.ppermute(upper_sent, "nrn", cross)
    merged = call(
        merge_kernel, shape(KT * 16, BF16), [vmem()] * 5,
        scratch=[pltpu.VMEM((KT * 16, VOX), F32)], name="merge", limit=4,
    )(odd, upper_new, lower_back, upper_other, lower_other)

    frames_new = new[:KT].reshape(KT, NF, PC)[:, :, 0].reshape(KT, NF // 2, 2)
    updated = jnp.where(core == 0, frames_new[:, :, 0], frames_new[:, :, 1])
    return updated[None], merged.reshape(KT, 16, VOX)


def solution(mesh):
    placed = (
        P("nrn", "tile", None, None),
        P("nrn", "tile", None),
        P("tile", None, None),
        P("tile", None),
        P("nrn", "tile", None),
        P("tile"),
    )
    return jax.shard_map(
        shards,
        mesh=mesh,
        in_specs=placed,
        out_specs=(P("nrn", "tile", None), P("tile", None, None)),
        check_vma=False,
    )
```

```python
import jax
import jax.numpy as jnp
from jax import lax
from jax.experimental import pallas as pl
from jax.experimental.pallas import tpu as pltpu
from jax.sharding import PartitionSpec as P

Z = 32
PR = 8
PC = 16
VOX = PR * PC
CHUNKS = 2
BAND = 224
NF = 8
KT = 96
NH = 2 * KT
NA = 4
XC = 32
TILES = NA * NH
FIELD = Z * XC
PADF = 4 * XC
EPSILON = 1e-06
MIB = 1024 * 1024

F32 = jnp.float32
BF16 = jnp.bfloat16


def iota(shape, dim):
    return lax.broadcasted_iota(jnp.int32, shape, dim)


def vmem():
    return pl.BlockSpec(memory_space=pltpu.VMEM)


def smem():
    return pl.BlockSpec(memory_space=pltpu.SMEM)


def call(kernel, out_shape, in_specs, scratch=(), name=None, limit=24, out_specs=None, aliases=None):
    if out_specs is None:
        out_specs = [vmem() for _ in out_shape] if isinstance(out_shape, (list, tuple)) else vmem()
    return pl.pallas_call(
        kernel,
        out_shape=out_shape,
        in_specs=in_specs,
        out_specs=out_specs,
        scratch_shapes=list(scratch),
        input_output_aliases=aliases or {},
        compiler_params=pltpu.CompilerParams(vmem_limit_bytes=limit * MIB),
        name=name,
    )


def places(block_ref):
    first = block_ref[...]
    ones = jnp.where(iota((16, VOX), 0) == 0, 1.0, 0.0).astype(BF16)

    def down_rows(values):
        return lax.dot_general(
            values.astype(F32).astype(BF16), ones, (((0,), (0,)), ((), ())), preferred_element_type=F32
        )

    plane = down_rows(first // 128)
    column = down_rows(first % 64).astype(jnp.int32)
    odd = (column + lax.axis_index("nrn")) % 2
    return plane, (column + odd) // 2, odd


def pick_rows(d, count_ref, odd, foot_ref, out_ref, wide):
    wide[...] = foot_ref[...].astype(F32)
    live = iota((KT, VOX), 0) < count_ref[0]
    for a in range(NA):
        left = wide[pl.ds(4 * a + 2 * d, KT, stride=16), :]
        right = wide[pl.ds(4 * a + 2 * d + 1, KT, stride=16), :]
        value = jnp.where(live, jnp.where(odd > 0, right, left), 0.0)
        out_ref[a * KT : (a + 1) * KT, :] = value.astype(BF16)


def rows_kernel(count_ref, block_ref, foot_ref, packet_ref, wide):
    plane, place, odd = places(block_ref)
    info = jnp.where(iota((KT, VOX), 1) < 64, plane, place.astype(F32))
    packet_ref[NA * KT : NA * KT + KT, :] = info.astype(BF16)
    pick_rows(1, count_ref, odd, foot_ref, packet_ref, wide)


def own_rows_kernel(count_ref, block_ref, foot_ref, packet_ref, upper_ref, odd_ref, wide):
    odd = places(block_ref)[2]
    odd_ref[...] = odd
    pick_rows(0, count_ref, odd, foot_ref, upper_ref, wide)


def register_kernel(shift_ref, movie_ref, out_ref, image, laid, load_sem, store_sem):
    height, width = movie_ref.shape
    bands = [(lo, min(height, lo + BAND)) for lo in range(0, height, BAND)]
    edges = [0] + [min(height, hi + 16) for _, hi in bands]
    loads = []
    for b in range(len(bands)):
        rows = pl.ds(edges[b], edges[b + 1] - edges[b])
        loads.append(pltpu.make_async_copy(movie_ref.at[rows, :], image.at[rows, :], load_sem.at[b]))
        loads[-1].start()
    s = shift_ref[0]
    u = shift_ref[1]
    groups = width // 256
    src = iota((512, 256), 0) - 128
    lane = iota((512, 256), 1) % 128
    want_column = (lane // PC) * 32 + (iota((512, 256), 1) // 128) * PC + lane % PC
    pick = jnp.where(src == want_column - u, 1.0, 0.0).astype(BF16)
    stores = []
    for b, (first, last) in enumerate(bands):
        loads[b].wait()
        lo = max(0, first - 16)
        hi = min(height, last + 16)
        want = iota((last - first, hi - lo), 0) + first - s
        have = iota((last - first, hi - lo), 1) + lo
        move = jnp.where(want == have, 1.0, 0.0).astype(BF16)
        rows = jnp.dot(move, image[lo:hi, :], preferred_element_type=F32).astype(BF16)
        parts = []
        for g in range(groups):
            start = max(0, 256 * g - 128)
            stop = min(width, 256 * g + 384)
            part = pick[start - 256 * g + 128 : stop - 256 * g + 128, :]
            parts.append(jnp.dot(rows[:, start:stop], part, preferred_element_type=F32))
        for t in range((last - first) // PR):
            for c in range(2):
                piece = [p[t * PR : (t + 1) * PR, c * 128 : (c + 1) * 128] for p in parts]
                at = ((first // PR + t) * 2 + c) * groups * PR
                laid[at : at + groups * PR, :] = jnp.concatenate(piece, axis=0).astype(BF16)
        where = pl.ds(first * 2 * groups, (last - first) * 2 * groups)
        stores.append(pltpu.make_async_copy(laid.at[where, :], out_ref.at[where, :], store_sem.at[b]))
        stores[-1].start()
    for copy in stores:
        copy.wait()


def tile_at(ref, block):
    return ref.at[pl.ds(pl.multiple_of(block * PR, PR), PR), :]


def expand(upper_ref, lower_ref, tiles_ref):
    lane_in = iota((VOX, PR * VOX), 0)
    lane_out = iota((VOX, PR * VOX), 1)
    same = (lane_in // PC == lane_out // VOX) & (lane_in % PC == lane_out % PC)
    spread = jnp.where(same, 1.0, 0.0).astype(BF16)
    for a in range(NA):
        for d, ref in ((0, upper_ref), (1, lower_ref)):
            rows = ref[a * KT : (a + 1) * KT, :]
            wide = jnp.dot(rows, spread, preferred_element_type=F32)
            base = (a * NH + d * KT) * PR
            for i in range(PR):
                tiles_ref[pl.ds(base + i, KT, stride=PR), :] = wide[:, i * VOX : (i + 1) * VOX]


def zero(ref, start, rows):
    step = 256

    def body(k, carry):
        ref[pl.ds(pl.multiple_of(start + k * step, step), step), :] = jnp.zeros((step, VOX), F32)
        return carry

    lax.fori_loop(0, rows // step, body, 0)


def clear(field_ref):
    zero(field_ref, 0, FIELD * PR)

    @pl.when(lax.axis_index("tile") == 0)
    def _():
        zero(field_ref, FIELD * PR, FIELD * PR)


def rebuild(place_ref, tiles_ref, trace_ref, field_ref):
    def body(n, carry):
        trace = jnp.broadcast_to(trace_ref[pl.ds(n, 1), :], (PR, VOX))
        base = place_ref[n]
        held = [tile_at(field_ref, base + a * XC)[...] for a in range(NA)]
        added = [tile_at(tiles_ref, a * NH + n)[...] * trace for a in range(NA)]
        for a in range(NA):
            tile_at(field_ref, base + a * XC)[...] = held[a] + added[a]
        return carry

    lax.fori_loop(0, NH, body, 0, unroll=8)


def project(place_ref, tiles_ref, field_ref, sums_ref):
    def body(n, carry):
        base = place_ref[n]
        total = tile_at(tiles_ref, n)[...] * tile_at(field_ref, base)[...]
        for a in range(1, NA):
            total = total + tile_at(tiles_ref, a * NH + n)[...] * tile_at(field_ref, base + a * XC)[...]
        tile_at(sums_ref, n)[...] = total
        return carry

    lax.fori_loop(0, NH, body, 0, unroll=8)
    rows = sums_ref[pl.ds(0, NH, stride=PR), :]
    for i in range(1, PR):
        rows = rows + sums_ref[pl.ds(i, NH, stride=PR), :]
    group = jnp.where(iota((VOX, VOX), 0) // PC == iota((VOX, VOX), 1) // PC, 1.0, 0.0)
    return jnp.dot(rows, group, preferred_element_type=F32, precision=lax.Precision.HIGHEST)


def denom_kernel(
    place_ref, upper_ref, packet_ref, trace_ref, tiles_ref, field, sums
):
    expand(upper_ref, packet_ref, tiles_ref)
    clear(field)
    rebuild(place_ref, tiles_ref, trace_ref, field)
    tiles_ref[TILES * PR : TILES * PR + NH, :] = project(place_ref, tiles_ref, field, sums)


def even_tile():
    return lax.bitwise_and(lax.axis_index("tile"), 1) == 0


def numer_kernel(place_ref, tiles_ref, image_ref, field_ref, sums_ref, permute_ref, sums):
    groups = XC // 8
    rows = groups * PR
    step = Z // CHUNKS
    chunk = step * NF * rows
    source = iota((VOX, NF * VOX), 0)
    target = iota((VOX, NF * VOX), 1)
    same = (source // PC == target // VOX) & (source % PC == target % PC)
    same = jnp.where(same, 1.0, 0.0).astype(BF16)
    frame = iota((16, NF * VOX), 1) % VOX // PC
    for f in range(NF):
        mine = jnp.where(frame == f, 1.0, 0.0).astype(BF16)
        for r in range(VOX // 16):
            at = f * VOX + 16 * r
            permute_ref[at : at + 16, :] = same[16 * r : 16 * r + 16, :] * mine
    for k in range(CHUNKS):
        lhs = []
        for z in range(step):
            start = k * chunk + z * NF * rows
            frames = [image_ref[start + f * rows : start + (f + 1) * rows, :] for f in range(NF)]
            lhs.append(jnp.concatenate(frames, axis=1))
        out = jnp.dot(jnp.concatenate(lhs, axis=0), permute_ref[...], preferred_element_type=F32)
        for z in range(step):
            for g in range(groups):
                for x in range(8):
                    at = z * rows + g * PR
                    to = ((k * step + z) * XC + g * 8 + x) * PR
                    field_ref[to : to + PR, :] = out[at : at + PR, x * VOX : (x + 1) * VOX]
    field_ref[FIELD * PR : (FIELD + PADF) * PR, :] = jnp.zeros((PADF * PR, VOX), F32)
    numer = project(place_ref, tiles_ref, field_ref, sums)
    denom = tiles_ref[TILES * PR : TILES * PR + NH, :]
    value = jnp.where(iota((NH, VOX), 1) % PC < PC // 2, numer, denom)
    upper, lower = value[:KT, :], value[KT:, :]
    even = even_tile()
    sums_ref[:KT, :] = jnp.where(even, lower, upper)
    sums_ref[KT:, :] = jnp.where(even, upper, lower)


def stage_kernel(spot_ref, image_ref, found_ref, field_ref):
    for d in range(2):
        def body(k, carry):
            spot = spot_ref[d * KT + k]
            for a in range(NA):
                tile_at(found_ref, (d * NA + a) * KT + k)[...] = tile_at(image_ref, spot + a * XC)[...]
            return carry

        lax.fori_loop(0, KT, body, 0, unroll=8)
    clear(field_ref)


def fold(start, tiles_ref, traces):
    lane_in = iota((2 * VOX, VOX), 0) % VOX
    lane_out = iota((2 * VOX, VOX), 1)
    total = None
    for i in range(PR):
        pick = jnp.where((lane_out // PC == i) & (lane_out % PC == lane_in % PC), 1.0, 0.0).astype(BF16)
        rows = tiles_ref[pl.ds(start * PR + i, NA * KT, stride=PR), :] * traces
        high = rows.astype(BF16)
        low = (rows - high.astype(F32)).astype(BF16)
        part = jnp.dot(jnp.concatenate([high, low], axis=1), pick, preferred_element_type=F32)
        total = part if total is None else total + part
    return total


def renew(d, place_ref, rows_ref, found_ref, field_ref, trace_ref, rebuilt):
    def body(k, carry):
        base = place_ref[d * KT + k]
        for a in range(NA):
            tile_at(rebuilt, a * KT + k)[...] = tile_at(field_ref, base + a * XC)[...]
        return carry

    lax.fori_loop(0, KT, body, 0, unroll=8)
    traces = jnp.concatenate([trace_ref[d * KT : (d + 1) * KT, :]] * NA, axis=0)
    ratio = fold(d * NA * KT, found_ref, traces) / (fold(0, rebuilt, traces) + EPSILON)
    return (rows_ref[0 : NA * KT, :].astype(F32) * ratio).astype(BF16)


def lower_kernel(
    place_ref, packet_ref, tiles_ref, found_ref, old_ref, mine_ref, near_ref, far_ref, cleared_ref,
    trace_ref, field_ref, out_ref, rebuilt,
):
    even = even_tile()
    first_mine, second_mine = mine_ref[:KT, :], mine_ref[KT:, :]
    near, far = near_ref[...], far_ref[...]
    upper = jnp.where(even, second_mine + near, first_mine + far)
    lower = jnp.where(even, first_mine + far, second_mine + near)
    sums = jnp.concatenate([upper, lower], axis=0)
    first = iota((NH, VOX), 1) % PC < PC // 2
    numer = jnp.where(first, sums, pltpu.roll(sums, PC // 2, 1))
    denom = jnp.where(first, pltpu.roll(sums, VOX - PC // 2, 1), sums)
    trace_ref[...] = old_ref[...] * numer / (denom + EPSILON)
    rebuild(place_ref, tiles_ref, trace_ref, field_ref)
    out_ref[...] = renew(1, place_ref, packet_ref, found_ref, field_ref, trace_ref, rebuilt)


def upper_kernel(place_ref, upper_ref, found_ref, field_ref, trace_ref, out_ref, sent_ref, rebuilt):
    value = renew(0, place_ref, upper_ref, found_ref, field_ref, trace_ref, rebuilt)
    out_ref[...] = value
    sent_ref[...] = value


def merge_kernel(odd_ref, upper_ref, lower_ref, upper_other, lower_other, out_ref, wide):
    odd = odd_ref[...] > 0
    for a in range(NA):
        rows = slice(a * KT, (a + 1) * KT)
        for d, mine_ref, other_ref in ((0, upper_ref, upper_other), (1, lower_ref, lower_other)):
            mine = mine_ref[rows, :].astype(F32)
            other = other_ref[rows, :].astype(F32)
            wide[pl.ds(4 * a + 2 * d, KT, stride=16), :] = jnp.where(odd, other, mine)
            wide[pl.ds(4 * a + 2 * d + 1, KT, stride=16), :] = jnp.where(odd, mine, other)
    out_ref[...] = wide[...].astype(BF16)


def shards(movie, shifts, footprints, blocks, traces, counts):
    tiles = lax.axis_size("tile")
    tile = lax.axis_index("tile")
    core = lax.axis_index("nrn")
    down = [(i, (i + 1) % tiles) for i in range(tiles)]
    up = [(j, i) for i, j in down]
    cross = [(0, 1), (1, 0)]

    def shape(rows, dtype):
        return jax.ShapeDtypeStruct((rows, VOX), dtype)

    mine = traces[0]
    above = lax.ppermute(mine, "tile", down)
    theirs = lax.ppermute(mine, "nrn", cross)

    hbm = pltpu.with_memory_space_constraint
    block_rows = hbm(blocks.T, pltpu.HBM)
    foot_rows = hbm(footprints.reshape(-1, VOX), pltpu.HBM)
    wide = pltpu.VMEM((KT * 16, VOX), F32)
    packet = call(
        rows_kernel, shape(NA * KT + KT, BF16), [smem(), vmem(), vmem()], scratch=[wide], name="rows", limit=4,
    )(counts, block_rows, foot_rows)
    packet_in = lax.ppermute(packet, "tile", down)

    height, width = movie.shape[2:]
    outside = pl.BlockSpec(memory_space=pltpu.HBM)
    sent = call(
        register_kernel, shape(tiles * 2 * XC, BF16), [smem(), outside],
        scratch=[
            pltpu.VMEM((height, width), BF16), pltpu.VMEM((tiles * 2 * XC, VOX), BF16),
            pltpu.SemaphoreType.DMA((5,)), pltpu.SemaphoreType.DMA((5,)),
        ],
        out_specs=outside, name="register", limit=12,
    )(hbm(shifts[0, 0], pltpu.HBM), hbm(movie[0, 0], pltpu.HBM))
    sent, packet_in, above, theirs = lax.optimization_barrier((sent, packet_in, above, theirs))
    images = lax.all_to_all(
        sent.reshape(tiles * 2, XC, VOX), ("tile", "nrn"), split_axis=0, concat_axis=0, tiled=True
    ).reshape(-1, VOX)

    upper, odd = call(
        own_rows_kernel, [pltpu.HBM((NA * KT, VOX), BF16), shape(KT, jnp.int32)],
        [smem(), vmem(), vmem(), pl.BlockSpec(memory_space=pl.ANY)], scratch=[wide], name="own_rows", limit=4,
    )(counts, block_rows, foot_rows, packet_in)

    both = jnp.concatenate([mine, above], axis=0)
    other = jnp.concatenate([theirs, lax.ppermute(above, "nrn", cross)], axis=0)
    frames = jnp.stack([jnp.where(core == 0, both, other), jnp.where(core == 0, other, both)], axis=-1)
    old = jnp.broadcast_to(frames.reshape(NH, NF)[:, :, None], (NH, NF, PC)).reshape(NH, VOX)

    def base_of(info):
        return info[NA * KT :, 0].astype(jnp.int32) * XC + info[NA * KT :, 64].astype(jnp.int32)

    base, base_in = base_of(packet), base_of(packet_in)
    margin = tile == 0
    place = jnp.concatenate([base, base_in + jnp.where(margin, FIELD, 0)])
    spot = jnp.concatenate([base, jnp.where(margin, FIELD, base_in)])

    field = pltpu.VMEM((2 * FIELD * PR, VOX), F32)
    sums = pltpu.VMEM((NH * PR, VOX), F32)
    in_vmem = pltpu.with_memory_space_constraint
    tiles_e = call(
        denom_kernel, pltpu.VMEM((TILES * PR + NH, VOX), F32), [smem()] + [vmem()] * 3,
        scratch=[field, sums], name="denominator", limit=14,
    )(place, upper, packet_in, old)
    tiles_e = in_vmem(tiles_e, pltpu.VMEM)
    image_field, partial = call(
        numer_kernel, [pltpu.VMEM(((FIELD + PADF) * PR, VOX), F32), shape(NH, F32)],
        [smem(), vmem(), vmem()],
        scratch=[pltpu.VMEM((NF * VOX, NF * VOX), BF16), sums],
        name="numerator", limit=12,
    )(spot, tiles_e, in_vmem(images, pltpu.VMEM))
    image_field = in_vmem(image_field, pltpu.VMEM)

    everyone = ("tile", "nrn")

    def other_core(pairs):
        return [(2 * i + c, 2 * j + 1 - c) for i, j in pairs for c in (0, 1)]

    partial = partial + lax.ppermute(partial, "nrn", cross)
    near = [(i, i ^ 1) for i in range(tiles)]
    far = [(i, (i - 1 + 2 * (i % 2)) % tiles) for i in range(tiles)]
    from_far = lax.ppermute(partial[:KT], "tile", far)
    from_near = lax.ppermute(partial[KT:], "tile", near)

    image_field, _ = lax.optimization_barrier((image_field, partial))
    found, cleared = call(
        stage_kernel, [pltpu.VMEM((TILES * PR, VOX), F32), pltpu.VMEM((2 * FIELD * PR, VOX), F32)],
        [smem(), vmem()], name="stage", limit=4,
    )(spot, in_vmem(image_field, pltpu.VMEM))
    found, cleared = in_vmem(found, pltpu.VMEM), in_vmem(cleared, pltpu.VMEM)
    half = pltpu.VMEM((NA * KT * PR, VOX), F32)
    new, rebuilt, lower_new = call(
        lower_kernel,
        [shape(NH, F32), pltpu.VMEM((2 * FIELD * PR, VOX), F32), shape(NA * KT, BF16)],
        [smem()] + [vmem()] * 8,
        scratch=[half], name="lower", limit=8, aliases={8: 1},
    )(place, packet_in, tiles_e, found, old, partial, from_near, from_far, cleared)
    lower_back = lax.ppermute(lower_new, "tile", up)
    lower_other = lax.ppermute(lower_new, everyone, other_core(up))
    upper_new, upper_sent = call(
        upper_kernel, [shape(NA * KT, BF16)] * 2, [smem()] + [vmem()] * 4,
        scratch=[half], name="upper", limit=8,
    )(place, upper, found, in_vmem(rebuilt, pltpu.VMEM), new)
    upper_other = lax.ppermute(upper_sent, "nrn", cross)
    merged = call(
        merge_kernel, shape(KT * 16, BF16), [vmem()] * 5,
        scratch=[pltpu.VMEM((KT * 16, VOX), F32)], name="merge", limit=4,
    )(odd, upper_new, lower_back, upper_other, lower_other)

    frames_new = new[:KT].reshape(KT, NF, PC)[:, :, 0].reshape(KT, NF // 2, 2)
    updated = jnp.where(core == 0, frames_new[:, :, 0], frames_new[:, :, 1])
    return updated[None], merged.reshape(KT, 16, VOX)


def solution(mesh):
    placed = (
        P("nrn", "tile", None, None),
        P("nrn", "tile", None),
        P("tile", None, None),
        P("tile", None),
        P("nrn", "tile", None),
        P("tile"),
    )
    return jax.shard_map(
        shards,
        mesh=mesh,
        in_specs=placed,
        out_specs=(P("nrn", "tile", None), P("tile", None, None)),
        check_vma=False,
    )
```

```python
import jax
import jax.numpy as jnp
from jax import lax
from jax.experimental import pallas as pl
from jax.experimental.pallas import tpu as pltpu
from jax.sharding import PartitionSpec as P

Z = 32
PR = 8
PC = 16
VOX = PR * PC
ROWS = 16
CHUNKS = 2
BAND = 224
NF = 8
KT = 96
NH = 2 * KT
NA = 4
XC = 32
TILES = NA * NH
FIELD = Z * XC
PADF = 4 * XC
EPSILON = 1e-06
MIB = 1024 * 1024

F32 = jnp.float32
BF16 = jnp.bfloat16


def iota(shape, dim):
    return lax.broadcasted_iota(jnp.int32, shape, dim)


def vmem():
    return pl.BlockSpec(memory_space=pltpu.VMEM)


def smem():
    return pl.BlockSpec(memory_space=pltpu.SMEM)


def call(kernel, out_shape, in_specs, scratch=(), name=None, limit=24, out_specs=None, aliases=None):
    if out_specs is None:
        out_specs = [vmem() for _ in out_shape] if isinstance(out_shape, (list, tuple)) else vmem()
    return pl.pallas_call(
        kernel,
        out_shape=out_shape,
        in_specs=in_specs,
        out_specs=out_specs,
        scratch_shapes=list(scratch),
        input_output_aliases=aliases or {},
        compiler_params=pltpu.CompilerParams(vmem_limit_bytes=limit * MIB),
        name=name,
    )


def places(block_ref):
    first = block_ref[...]
    ones = jnp.where(iota((16, VOX), 0) == 0, 1.0, 0.0).astype(BF16)

    def down_rows(values):
        return lax.dot_general(
            values.astype(F32).astype(BF16), ones, (((0,), (0,)), ((), ())), preferred_element_type=F32
        )

    plane = down_rows(first // 128)
    column = down_rows(first % 64).astype(jnp.int32)
    odd = (column + lax.axis_index("nrn")) % 2
    return plane, (column + odd) // 2, odd


def pick_rows(d, count_ref, odd, foot_ref, out_ref, wide):
    wide[...] = foot_ref[...].astype(F32)
    live = iota((KT, VOX), 0) < count_ref[0]
    for a in range(NA):
        left = wide[pl.ds(4 * a + 2 * d, KT, stride=16), :]
        right = wide[pl.ds(4 * a + 2 * d + 1, KT, stride=16), :]
        value = jnp.where(live, jnp.where(odd > 0, right, left), 0.0)
        out_ref[a * KT : (a + 1) * KT, :] = value.astype(BF16)


def rows_kernel(count_ref, block_ref, foot_ref, packet_ref, wide):
    plane, place, odd = places(block_ref)
    info = jnp.where(iota((KT, VOX), 1) < 64, plane, place.astype(F32))
    packet_ref[NA * KT : NA * KT + KT, :] = info.astype(BF16)
    pick_rows(1, count_ref, odd, foot_ref, packet_ref, wide)


def own_rows_kernel(count_ref, block_ref, foot_ref, packet_ref, upper_ref, odd_ref, wide):
    odd = places(block_ref)[2]
    odd_ref[...] = odd
    pick_rows(0, count_ref, odd, foot_ref, upper_ref, wide)


def register_kernel(shift_ref, movie_ref, out_ref, image, laid, load_sem, store_sem):
    height, width = movie_ref.shape
    bands = [(lo, min(height, lo + BAND)) for lo in range(0, height, BAND)]
    edges = [0] + [min(height, hi + 16) for _, hi in bands]
    loads = []
    for b in range(len(bands)):
        rows = pl.ds(edges[b], edges[b + 1] - edges[b])
        loads.append(pltpu.make_async_copy(movie_ref.at[rows, :], image.at[rows, :], load_sem.at[b]))
        loads[-1].start()
    s = shift_ref[0]
    u = shift_ref[1]
    groups = width // 256
    src = iota((512, 256), 0) - 128
    lane = iota((512, 256), 1) % 128
    want_column = (lane // PC) * 32 + (iota((512, 256), 1) // 128) * PC + lane % PC
    pick = jnp.where(src == want_column - u, 1.0, 0.0).astype(BF16)
    stores = []
    for b, (first, last) in enumerate(bands):
        loads[b].wait()
        lo = max(0, first - 16)
        hi = min(height, last + 16)
        want = iota((last - first, hi - lo), 0) + first - s
        have = iota((last - first, hi - lo), 1) + lo
        move = jnp.where(want == have, 1.0, 0.0).astype(BF16)
        rows = jnp.dot(move, image[lo:hi, :], preferred_element_type=F32).astype(BF16)
        parts = []
        for g in range(groups):
            start = max(0, 256 * g - 128)
            stop = min(width, 256 * g + 384)
            part = pick[start - 256 * g + 128 : stop - 256 * g + 128, :]
            parts.append(jnp.dot(rows[:, start:stop], part, preferred_element_type=F32))
        for t in range((last - first) // PR):
            for c in range(2):
                piece = [p[t * PR : (t + 1) * PR, c * 128 : (c + 1) * 128] for p in parts]
                at = ((first // PR + t) * 2 + c) * groups * PR
                laid[at : at + groups * PR, :] = jnp.concatenate(piece, axis=0).astype(BF16)
        where = pl.ds(first * 2 * groups, (last - first) * 2 * groups)
        stores.append(pltpu.make_async_copy(laid.at[where, :], out_ref.at[where, :], store_sem.at[b]))
        stores[-1].start()
    for copy in stores:
        copy.wait()


def tile_at(ref, block):
    return ref.at[pl.ds(pl.multiple_of(block * PR, PR), PR), :]


def expand(upper_ref, lower_ref, tiles_ref):
    lane_in = iota((VOX, PR * VOX), 0)
    lane_out = iota((VOX, PR * VOX), 1)
    same = (lane_in // PC == lane_out // VOX) & (lane_in % PC == lane_out % PC)
    spread = jnp.where(same, 1.0, 0.0).astype(BF16)
    for a in range(NA):
        for d, ref in ((0, upper_ref), (1, lower_ref)):
            rows = ref[a * KT : (a + 1) * KT, :]
            wide = jnp.dot(rows, spread, preferred_element_type=F32)
            base = (a * NH + d * KT) * PR
            for i in range(PR):
                tiles_ref[pl.ds(base + i, KT, stride=PR), :] = wide[:, i * VOX : (i + 1) * VOX]


def zero(ref, start, rows):
    step = 256

    def body(k, carry):
        ref[pl.ds(pl.multiple_of(start + k * step, step), step), :] = jnp.zeros((step, VOX), F32)
        return carry

    lax.fori_loop(0, rows // step, body, 0)


def clear(field_ref):
    zero(field_ref, 0, FIELD * PR)

    @pl.when(lax.axis_index("tile") == 0)
    def _():
        zero(field_ref, FIELD * PR, FIELD * PR)


def rebuild(place_ref, tiles_ref, trace_ref, field_ref):
    def body(n, carry):
        trace = jnp.broadcast_to(trace_ref[pl.ds(n, 1), :], (PR, VOX))
        base = place_ref[n]
        held = [tile_at(field_ref, base + a * XC)[...] for a in range(NA)]
        added = [tile_at(tiles_ref, a * NH + n)[...] * trace for a in range(NA)]
        for a in range(NA):
            tile_at(field_ref, base + a * XC)[...] = held[a] + added[a]
        return carry

    lax.fori_loop(0, NH, body, 0, unroll=8)


def project(place_ref, tiles_ref, field_ref, sums_ref):
    def body(n, carry):
        base = place_ref[n]
        total = tile_at(tiles_ref, n)[...] * tile_at(field_ref, base)[...]
        for a in range(1, NA):
            total = total + tile_at(tiles_ref, a * NH + n)[...] * tile_at(field_ref, base + a * XC)[...]
        tile_at(sums_ref, n)[...] = total
        return carry

    lax.fori_loop(0, NH, body, 0, unroll=8)
    rows = sums_ref[pl.ds(0, NH, stride=PR), :]
    for i in range(1, PR):
        rows = rows + sums_ref[pl.ds(i, NH, stride=PR), :]
    group = jnp.where(iota((VOX, VOX), 0) // PC == iota((VOX, VOX), 1) // PC, 1.0, 0.0)
    return jnp.dot(rows, group, preferred_element_type=F32, precision=lax.Precision.HIGHEST)


def denom_kernel(
    place_ref, upper_ref, packet_ref, trace_ref, tiles_ref, field, sums
):
    expand(upper_ref, packet_ref, tiles_ref)
    clear(field)
    rebuild(place_ref, tiles_ref, trace_ref, field)
    tiles_ref[TILES * PR : TILES * PR + NH, :] = project(place_ref, tiles_ref, field, sums)


def pack(rows):
    slot = iota((ROWS, VOX), 1) % 8
    packed = jnp.zeros((ROWS, VOX), F32)
    for j in range(KT // ROWS):
        packed = jnp.where(slot == j, rows[j * ROWS : (j + 1) * ROWS, :], packed)
    return packed


def unpack(packed, spread):
    high = packed.astype(BF16)
    rest = packed - high.astype(F32)
    middle = rest.astype(BF16)
    low = (rest - middle.astype(F32)).astype(BF16)
    wide = jnp.dot(jnp.concatenate([high, middle, low], axis=0), spread, preferred_element_type=F32)
    wide = wide[: 2 * ROWS] + wide[2 * ROWS : 4 * ROWS] + wide[4 * ROWS :]
    slots = KT // ROWS
    parts = []
    for kind in range(2):
        rows = []
        for d in range(2):
            for j in range(slots):
                at = (kind * slots + j) * VOX
                rows.append(wide[d * ROWS : (d + 1) * ROWS, at : at + VOX])
        parts.append(jnp.concatenate(rows, axis=0))
    return parts


def even_tile():
    return lax.bitwise_and(lax.axis_index("tile"), 1) == 0


def numer_kernel(place_ref, tiles_ref, image_ref, field_ref, sums_ref, permute_ref, sums):
    groups = XC // 8
    rows = groups * PR
    step = Z // CHUNKS
    chunk = step * NF * rows
    source = iota((VOX, NF * VOX), 0)
    target = iota((VOX, NF * VOX), 1)
    same = (source // PC == target // VOX) & (source % PC == target % PC)
    same = jnp.where(same, 1.0, 0.0).astype(BF16)
    frame = iota((16, NF * VOX), 1) % VOX // PC
    for f in range(NF):
        mine = jnp.where(frame == f, 1.0, 0.0).astype(BF16)
        for r in range(VOX // 16):
            at = f * VOX + 16 * r
            permute_ref[at : at + 16, :] = same[16 * r : 16 * r + 16, :] * mine
    for k in range(CHUNKS):
        lhs = []
        for z in range(step):
            start = k * chunk + z * NF * rows
            frames = [image_ref[start + f * rows : start + (f + 1) * rows, :] for f in range(NF)]
            lhs.append(jnp.concatenate(frames, axis=1))
        out = jnp.dot(jnp.concatenate(lhs, axis=0), permute_ref[...], preferred_element_type=F32)
        for z in range(step):
            for g in range(groups):
                for x in range(8):
                    at = z * rows + g * PR
                    to = ((k * step + z) * XC + g * 8 + x) * PR
                    field_ref[to : to + PR, :] = out[at : at + PR, x * VOX : (x + 1) * VOX]
    field_ref[FIELD * PR : (FIELD + PADF) * PR, :] = jnp.zeros((PADF * PR, VOX), F32)
    numer = project(place_ref, tiles_ref, field_ref, sums)
    denom = tiles_ref[TILES * PR : TILES * PR + NH, :]
    value = jnp.where(iota((NH, VOX), 1) % PC < PC // 2, numer, denom)
    upper, lower = pack(value[:KT, :]), pack(value[KT:, :])
    even = even_tile()
    sums_ref[:ROWS, :] = jnp.where(even, lower, upper)
    sums_ref[ROWS:, :] = jnp.where(even, upper, lower)


def stage_kernel(spot_ref, image_ref, found_ref, field_ref, spread_ref):
    source = iota((VOX, VOX), 0)
    group = source // PC == iota((VOX, VOX), 1) // PC
    slots = KT // ROWS
    for kind in range(2):
        for j in range(slots):
            at = (kind * slots + j) * VOX
            pick = group & (source % PC == kind * 8 + j)
            spread_ref[:, at : at + VOX] = jnp.where(pick, 1.0, 0.0).astype(BF16)
    for d in range(2):
        def body(k, carry):
            spot = spot_ref[d * KT + k]
            for a in range(NA):
                tile_at(found_ref, (d * NA + a) * KT + k)[...] = tile_at(image_ref, spot + a * XC)[...]
            return carry

        lax.fori_loop(0, KT, body, 0, unroll=8)
    clear(field_ref)


def fold(start, tiles_ref, traces):
    lane_in = iota((2 * VOX, VOX), 0) % VOX
    lane_out = iota((2 * VOX, VOX), 1)
    total = None
    for i in range(PR):
        pick = jnp.where((lane_out // PC == i) & (lane_out % PC == lane_in % PC), 1.0, 0.0).astype(BF16)
        rows = tiles_ref[pl.ds(start * PR + i, NA * KT, stride=PR), :] * traces
        high = rows.astype(BF16)
        low = (rows - high.astype(F32)).astype(BF16)
        part = jnp.dot(jnp.concatenate([high, low], axis=1), pick, preferred_element_type=F32)
        total = part if total is None else total + part
    return total


def renew(d, place_ref, rows_ref, found_ref, field_ref, trace_ref, rebuilt):
    def body(k, carry):
        base = place_ref[d * KT + k]
        for a in range(NA):
            tile_at(rebuilt, a * KT + k)[...] = tile_at(field_ref, base + a * XC)[...]
        return carry

    lax.fori_loop(0, KT, body, 0, unroll=8)
    traces = jnp.concatenate([trace_ref[d * KT : (d + 1) * KT, :]] * NA, axis=0)
    ratio = fold(d * NA * KT, found_ref, traces) / (fold(0, rebuilt, traces) + EPSILON)
    return (rows_ref[0 : NA * KT, :].astype(F32) * ratio).astype(BF16)


def lower_kernel(
    place_ref, packet_ref, tiles_ref, found_ref, old_ref, mine_ref, near_ref, far_ref, spread_ref, cleared_ref,
    trace_ref, field_ref, out_ref, rebuilt,
):
    even = even_tile()
    first = mine_ref[:ROWS, :] + far_ref[...]
    second = mine_ref[ROWS:, :] + near_ref[...]
    upper = jnp.where(even, second, first)
    lower = jnp.where(even, first, second)
    numer, denom = unpack(jnp.concatenate([upper, lower], axis=0), spread_ref[...])
    trace_ref[...] = old_ref[...] * numer / (denom + EPSILON)
    rebuild(place_ref, tiles_ref, trace_ref, field_ref)
    out_ref[...] = renew(1, place_ref, packet_ref, found_ref, field_ref, trace_ref, rebuilt)


def upper_kernel(place_ref, upper_ref, found_ref, field_ref, trace_ref, out_ref, sent_ref, rebuilt):
    value = renew(0, place_ref, upper_ref, found_ref, field_ref, trace_ref, rebuilt)
    out_ref[...] = value
    sent_ref[...] = value


def merge_kernel(odd_ref, upper_ref, lower_ref, upper_other, lower_other, out_ref, wide):
    odd = odd_ref[...] > 0
    for a in range(NA):
        rows = slice(a * KT, (a + 1) * KT)
        for d, mine_ref, other_ref in ((0, upper_ref, upper_other), (1, lower_ref, lower_other)):
            mine = mine_ref[rows, :].astype(F32)
            other = other_ref[rows, :].astype(F32)
            wide[pl.ds(4 * a + 2 * d, KT, stride=16), :] = jnp.where(odd, other, mine)
            wide[pl.ds(4 * a + 2 * d + 1, KT, stride=16), :] = jnp.where(odd, mine, other)
    out_ref[...] = wide[...].astype(BF16)


def shards(movie, shifts, footprints, blocks, traces, counts):
    tiles = lax.axis_size("tile")
    tile = lax.axis_index("tile")
    core = lax.axis_index("nrn")
    down = [(i, (i + 1) % tiles) for i in range(tiles)]
    up = [(j, i) for i, j in down]
    cross = [(0, 1), (1, 0)]

    def shape(rows, dtype):
        return jax.ShapeDtypeStruct((rows, VOX), dtype)

    mine = traces[0]
    above = lax.ppermute(mine, "tile", down)
    theirs = lax.ppermute(mine, "nrn", cross)

    hbm = pltpu.with_memory_space_constraint
    block_rows = hbm(blocks.T, pltpu.HBM)
    foot_rows = hbm(footprints.reshape(-1, VOX), pltpu.HBM)
    wide = pltpu.VMEM((KT * 16, VOX), F32)
    packet = call(
        rows_kernel, shape(NA * KT + KT, BF16), [smem(), vmem(), vmem()], scratch=[wide], name="rows", limit=4,
    )(counts, block_rows, foot_rows)
    packet_in = lax.ppermute(packet, "tile", down)

    height, width = movie.shape[2:]
    outside = pl.BlockSpec(memory_space=pltpu.HBM)
    sent = call(
        register_kernel, shape(tiles * 2 * XC, BF16), [smem(), outside],
        scratch=[
            pltpu.VMEM((height, width), BF16), pltpu.VMEM((tiles * 2 * XC, VOX), BF16),
            pltpu.SemaphoreType.DMA((5,)), pltpu.SemaphoreType.DMA((5,)),
        ],
        out_specs=outside, name="register", limit=12,
    )(hbm(shifts[0, 0], pltpu.HBM), hbm(movie[0, 0], pltpu.HBM))
    sent, packet_in, above, theirs = lax.optimization_barrier((sent, packet_in, above, theirs))
    images = lax.all_to_all(
        sent.reshape(tiles * 2, XC, VOX), ("tile", "nrn"), split_axis=0, concat_axis=0, tiled=True
    ).reshape(-1, VOX)

    upper, odd = call(
        own_rows_kernel, [pltpu.HBM((NA * KT, VOX), BF16), shape(KT, jnp.int32)],
        [smem(), vmem(), vmem(), pl.BlockSpec(memory_space=pl.ANY)], scratch=[wide], name="own_rows", limit=4,
    )(counts, block_rows, foot_rows, packet_in)

    both = jnp.concatenate([mine, above], axis=0)
    other = jnp.concatenate([theirs, lax.ppermute(above, "nrn", cross)], axis=0)
    frames = jnp.stack([jnp.where(core == 0, both, other), jnp.where(core == 0, other, both)], axis=-1)
    old = jnp.broadcast_to(frames.reshape(NH, NF)[:, :, None], (NH, NF, PC)).reshape(NH, VOX)

    def base_of(info):
        return info[NA * KT :, 0].astype(jnp.int32) * XC + info[NA * KT :, 64].astype(jnp.int32)

    base, base_in = base_of(packet), base_of(packet_in)
    margin = tile == 0
    place = jnp.concatenate([base, base_in + jnp.where(margin, FIELD, 0)])
    spot = jnp.concatenate([base, jnp.where(margin, FIELD, base_in)])

    field = pltpu.VMEM((2 * FIELD * PR, VOX), F32)
    sums = pltpu.VMEM((NH * PR, VOX), F32)
    in_vmem = pltpu.with_memory_space_constraint
    tiles_e = call(
        denom_kernel, pltpu.VMEM((TILES * PR + NH, VOX), F32), [smem()] + [vmem()] * 3,
        scratch=[field, sums], name="denominator", limit=14,
    )(place, upper, packet_in, old)
    tiles_e = in_vmem(tiles_e, pltpu.VMEM)
    image_field, partial = call(
        numer_kernel, [pltpu.VMEM(((FIELD + PADF) * PR, VOX), F32), shape(2 * ROWS, F32)],
        [smem(), vmem(), vmem()],
        scratch=[pltpu.VMEM((NF * VOX, NF * VOX), BF16), sums],
        name="numerator", limit=12,
    )(spot, tiles_e, in_vmem(images, pltpu.VMEM))
    image_field = in_vmem(image_field, pltpu.VMEM)

    everyone = ("tile", "nrn")

    def other_core(pairs):
        return [(2 * i + c, 2 * j + 1 - c) for i, j in pairs for c in (0, 1)]

    partial = partial + lax.ppermute(partial, "nrn", cross)
    near = [(i, i ^ 1) for i in range(tiles)]
    far = [(i, (i - 1 + 2 * (i % 2)) % tiles) for i in range(tiles)]
    from_far = lax.ppermute(partial[:ROWS], "tile", far)
    from_near = lax.ppermute(partial[ROWS:], "tile", near)

    image_field, _ = lax.optimization_barrier((image_field, partial))
    found, cleared, spread = call(
        stage_kernel,
        [
            pltpu.VMEM((TILES * PR, VOX), F32), pltpu.VMEM((2 * FIELD * PR, VOX), F32),
            pltpu.VMEM((VOX, 2 * KT // ROWS * VOX), BF16),
        ],
        [smem(), vmem()], name="stage", limit=4,
    )(spot, in_vmem(image_field, pltpu.VMEM))
    found, cleared, spread = [in_vmem(v, pltpu.VMEM) for v in (found, cleared, spread)]
    half = pltpu.VMEM((NA * KT * PR, VOX), F32)
    new, rebuilt, lower_new = call(
        lower_kernel,
        [shape(NH, F32), pltpu.VMEM((2 * FIELD * PR, VOX), F32), shape(NA * KT, BF16)],
        [smem()] + [vmem()] * 9,
        scratch=[half], name="lower", limit=8, aliases={9: 1},
    )(place, packet_in, tiles_e, found, old, partial, from_near, from_far, spread, cleared)
    lower_back = lax.ppermute(lower_new, "tile", up)
    lower_other = lax.ppermute(lower_new, everyone, other_core(up))
    upper_new, upper_sent = call(
        upper_kernel, [shape(NA * KT, BF16)] * 2, [smem()] + [vmem()] * 4,
        scratch=[half], name="upper", limit=8,
    )(place, upper, found, in_vmem(rebuilt, pltpu.VMEM), new)
    upper_other = lax.ppermute(upper_sent, "nrn", cross)
    merged = call(
        merge_kernel, shape(KT * 16, BF16), [vmem()] * 5,
        scratch=[pltpu.VMEM((KT * 16, VOX), F32)], name="merge", limit=4,
    )(odd, upper_new, lower_back, upper_other, lower_other)

    frames_new = new[:KT].reshape(KT, NF, PC)[:, :, 0].reshape(KT, NF // 2, 2)
    updated = jnp.where(core == 0, frames_new[:, :, 0], frames_new[:, :, 1])
    return updated[None], merged.reshape(KT, 16, VOX)


def solution(mesh):
    placed = (
        P("nrn", "tile", None, None),
        P("nrn", "tile", None),
        P("tile", None, None),
        P("tile", None),
        P("nrn", "tile", None),
        P("tile"),
    )
    return jax.shard_map(
        shards,
        mesh=mesh,
        in_specs=placed,
        out_specs=(P("nrn", "tile", None), P("tile", None, None)),
        check_vma=False,
    )
```

```python
import jax
import jax.numpy as jnp
from jax import lax
from jax.experimental import pallas as pl
from jax.experimental.pallas import tpu as pltpu
from jax.sharding import PartitionSpec as P

Z = 32
PR = 8
PC = 16
VOX = PR * PC
ROWS = 16
CHUNKS = 2
BAND = 224
NF = 8
KT = 96
NH = 2 * KT
NA = 4
XC = 32
TILES = NA * NH
FIELD = Z * XC
PADF = 4 * XC
EPSILON = 1e-06
MIB = 1024 * 1024

F32 = jnp.float32
BF16 = jnp.bfloat16


def iota(shape, dim):
    return lax.broadcasted_iota(jnp.int32, shape, dim)


def vmem():
    return pl.BlockSpec(memory_space=pltpu.VMEM)


def smem():
    return pl.BlockSpec(memory_space=pltpu.SMEM)


def call(kernel, out_shape, in_specs, scratch=(), name=None, limit=24, out_specs=None, aliases=None):
    if out_specs is None:
        out_specs = [vmem() for _ in out_shape] if isinstance(out_shape, (list, tuple)) else vmem()
    return pl.pallas_call(
        kernel,
        out_shape=out_shape,
        in_specs=in_specs,
        out_specs=out_specs,
        scratch_shapes=list(scratch),
        input_output_aliases=aliases or {},
        compiler_params=pltpu.CompilerParams(vmem_limit_bytes=limit * MIB),
        name=name,
    )


def places(block_ref):
    first = block_ref[...]
    ones = jnp.where(iota((16, VOX), 0) == 0, 1.0, 0.0).astype(BF16)

    def down_rows(values):
        return lax.dot_general(
            values.astype(F32).astype(BF16), ones, (((0,), (0,)), ((), ())), preferred_element_type=F32
        )

    plane = down_rows(first // 128)
    column = down_rows(first % 64).astype(jnp.int32)
    odd = (column + lax.axis_index("nrn")) % 2
    return plane, (column + odd) // 2, odd


def pick_rows(d, count_ref, odd, foot_ref, out_ref, wide):
    wide[...] = foot_ref[...].astype(F32)
    live = iota((KT, VOX), 0) < count_ref[0]
    for a in range(NA):
        left = wide[pl.ds(4 * a + 2 * d, KT, stride=16), :]
        right = wide[pl.ds(4 * a + 2 * d + 1, KT, stride=16), :]
        value = jnp.where(live, jnp.where(odd > 0, right, left), 0.0)
        out_ref[a * KT : (a + 1) * KT, :] = value.astype(BF16)


def rows_kernel(count_ref, block_ref, foot_ref, packet_ref, wide):
    plane, place, odd = places(block_ref)
    info = jnp.where(iota((KT, VOX), 1) < 64, plane, place.astype(F32))
    packet_ref[NA * KT : NA * KT + KT, :] = info.astype(BF16)
    pick_rows(1, count_ref, odd, foot_ref, packet_ref, wide)


def own_rows_kernel(count_ref, block_ref, foot_ref, packet_ref, upper_ref, odd_ref, wide):
    odd = places(block_ref)[2]
    odd_ref[...] = odd
    pick_rows(0, count_ref, odd, foot_ref, upper_ref, wide)


def register_kernel(shift_ref, movie_ref, out_ref, image, laid, load_sem, store_sem):
    height, width = movie_ref.shape
    bands = [(lo, min(height, lo + BAND)) for lo in range(0, height, BAND)]
    edges = [0] + [min(height, hi + 16) for _, hi in bands]
    loads = []
    for b in range(len(bands)):
        rows = pl.ds(edges[b], edges[b + 1] - edges[b])
        loads.append(pltpu.make_async_copy(movie_ref.at[rows, :], image.at[rows, :], load_sem.at[b]))
        loads[-1].start()
    s = shift_ref[0]
    u = shift_ref[1]
    groups = width // 256
    src = iota((512, 256), 0) - 128
    lane = iota((512, 256), 1) % 128
    want_column = (lane // PC) * 32 + (iota((512, 256), 1) // 128) * PC + lane % PC
    pick = jnp.where(src == want_column - u, 1.0, 0.0).astype(BF16)
    stores = []
    for b, (first, last) in enumerate(bands):
        loads[b].wait()
        lo = max(0, first - 16)
        hi = min(height, last + 16)
        want = iota((last - first, hi - lo), 0) + first - s
        have = iota((last - first, hi - lo), 1) + lo
        move = jnp.where(want == have, 1.0, 0.0).astype(BF16)
        rows = jnp.dot(move, image[lo:hi, :], preferred_element_type=F32).astype(BF16)
        parts = []
        for g in range(groups):
            start = max(0, 256 * g - 128)
            stop = min(width, 256 * g + 384)
            part = pick[start - 256 * g + 128 : stop - 256 * g + 128, :]
            parts.append(jnp.dot(rows[:, start:stop], part, preferred_element_type=F32))
        for t in range((last - first) // PR):
            for c in range(2):
                piece = [p[t * PR : (t + 1) * PR, c * 128 : (c + 1) * 128] for p in parts]
                at = ((first // PR + t) * 2 + c) * groups * PR
                laid[at : at + groups * PR, :] = jnp.concatenate(piece, axis=0).astype(BF16)
        where = pl.ds(first * 2 * groups, (last - first) * 2 * groups)
        stores.append(pltpu.make_async_copy(laid.at[where, :], out_ref.at[where, :], store_sem.at[b]))
        stores[-1].start()
    for copy in stores:
        copy.wait()


def tile_at(ref, block):
    return ref.at[pl.ds(pl.multiple_of(block * PR, PR), PR), :]


def expand(upper_ref, lower_ref, tiles_ref):
    lane_in = iota((VOX, PR * VOX), 0)
    lane_out = iota((VOX, PR * VOX), 1)
    same = (lane_in // PC == lane_out // VOX) & (lane_in % PC == lane_out % PC)
    spread = jnp.where(same, 1.0, 0.0).astype(BF16)
    for a in range(NA):
        for d, ref in ((0, upper_ref), (1, lower_ref)):
            rows = ref[a * KT : (a + 1) * KT, :]
            wide = jnp.dot(rows, spread, preferred_element_type=F32)
            base = (a * NH + d * KT) * PR
            for i in range(PR):
                tiles_ref[pl.ds(base + i, KT, stride=PR), :] = wide[:, i * VOX : (i + 1) * VOX]


def zero(ref, start, rows):
    step = 256

    def body(k, carry):
        ref[pl.ds(pl.multiple_of(start + k * step, step), step), :] = jnp.zeros((step, VOX), F32)
        return carry

    lax.fori_loop(0, rows // step, body, 0)


def clear(field_ref):
    zero(field_ref, 0, FIELD * PR)

    @pl.when(lax.axis_index("tile") == 0)
    def _():
        zero(field_ref, FIELD * PR, FIELD * PR)


def rebuild(place_ref, tiles_ref, trace_ref, field_ref):
    def body(n, carry):
        trace = jnp.broadcast_to(trace_ref[pl.ds(n, 1), :], (PR, VOX))
        base = place_ref[n]
        held = [tile_at(field_ref, base + a * XC)[...] for a in range(NA)]
        added = [tile_at(tiles_ref, a * NH + n)[...] * trace for a in range(NA)]
        for a in range(NA):
            tile_at(field_ref, base + a * XC)[...] = held[a] + added[a]
        return carry

    lax.fori_loop(0, NH, body, 0, unroll=8)


def project(place_ref, tiles_ref, field_ref, sums_ref):
    def body(n, carry):
        base = place_ref[n]
        total = tile_at(tiles_ref, n)[...] * tile_at(field_ref, base)[...]
        for a in range(1, NA):
            total = total + tile_at(tiles_ref, a * NH + n)[...] * tile_at(field_ref, base + a * XC)[...]
        tile_at(sums_ref, n)[...] = total
        return carry

    lax.fori_loop(0, NH, body, 0, unroll=8)
    rows = sums_ref[pl.ds(0, NH, stride=PR), :]
    for i in range(1, PR):
        rows = rows + sums_ref[pl.ds(i, NH, stride=PR), :]
    group = jnp.where(iota((VOX, VOX), 0) // PC == iota((VOX, VOX), 1) // PC, 1.0, 0.0)
    return jnp.dot(rows, group, preferred_element_type=F32, precision=lax.Precision.HIGHEST)


def denom_kernel(
    place_ref, upper_ref, packet_ref, trace_ref, tiles_ref, field, sums
):
    expand(upper_ref, packet_ref, tiles_ref)
    clear(field)
    rebuild(place_ref, tiles_ref, trace_ref, field)
    tiles_ref[TILES * PR : TILES * PR + NH, :] = project(place_ref, tiles_ref, field, sums)


def pack(rows):
    slot = iota((ROWS, VOX), 1) % 8
    packed = jnp.zeros((ROWS, VOX), F32)
    for j in range(KT // ROWS):
        packed = jnp.where(slot == j, rows[j * ROWS : (j + 1) * ROWS, :], packed)
    return packed


def unpack(packed, spread):
    high = packed.astype(BF16)
    rest = packed - high.astype(F32)
    middle = rest.astype(BF16)
    low = (rest - middle.astype(F32)).astype(BF16)
    wide = jnp.dot(jnp.concatenate([high, middle, low], axis=0), spread, preferred_element_type=F32)
    wide = wide[: 2 * ROWS] + wide[2 * ROWS : 4 * ROWS] + wide[4 * ROWS :]
    slots = KT // ROWS
    parts = []
    for kind in range(2):
        rows = []
        for d in range(2):
            for j in range(slots):
                at = (kind * slots + j) * VOX
                rows.append(wide[d * ROWS : (d + 1) * ROWS, at : at + VOX])
        parts.append(jnp.concatenate(rows, axis=0))
    return parts


def even_tile():
    return lax.bitwise_and(lax.axis_index("tile"), 1) == 0


def numer_kernel(place_ref, tiles_ref, image_ref, field_ref, sums_ref, permute_ref, sums):
    groups = XC // 8
    rows = groups * PR
    step = Z // CHUNKS
    chunk = step * NF * rows
    source = iota((VOX, NF * VOX), 0)
    target = iota((VOX, NF * VOX), 1)
    same = (source // PC == target // VOX) & (source % PC == target % PC)
    same = jnp.where(same, 1.0, 0.0).astype(BF16)
    frame = iota((16, NF * VOX), 1) % VOX // PC
    for f in range(NF):
        mine = jnp.where(frame == f, 1.0, 0.0).astype(BF16)
        for r in range(VOX // 16):
            at = f * VOX + 16 * r
            permute_ref[at : at + 16, :] = same[16 * r : 16 * r + 16, :] * mine
    for k in range(CHUNKS):
        lhs = []
        for z in range(step):
            start = k * chunk + z * NF * rows
            frames = [image_ref[start + f * rows : start + (f + 1) * rows, :] for f in range(NF)]
            lhs.append(jnp.concatenate(frames, axis=1))
        out = jnp.dot(jnp.concatenate(lhs, axis=0), permute_ref[...], preferred_element_type=F32)
        for z in range(step):
            for g in range(groups):
                for x in range(8):
                    at = z * rows + g * PR
                    to = ((k * step + z) * XC + g * 8 + x) * PR
                    field_ref[to : to + PR, :] = out[at : at + PR, x * VOX : (x + 1) * VOX]
    field_ref[FIELD * PR : (FIELD + PADF) * PR, :] = jnp.zeros((PADF * PR, VOX), F32)
    numer = project(place_ref, tiles_ref, field_ref, sums)
    denom = tiles_ref[TILES * PR : TILES * PR + NH, :]
    value = jnp.where(iota((NH, VOX), 1) % PC < PC // 2, numer, denom)
    upper, lower = pack(value[:KT, :]), pack(value[KT:, :])
    even = even_tile()
    sums_ref[:ROWS, :] = jnp.where(even, lower, upper)
    sums_ref[ROWS:, :] = jnp.where(even, upper, lower)


def stage_kernel(spot_ref, image_ref, found_ref, field_ref, spread_ref):
    source = iota((VOX, VOX), 0)
    group = source // PC == iota((VOX, VOX), 1) // PC
    slots = KT // ROWS
    for kind in range(2):
        for j in range(slots):
            at = (kind * slots + j) * VOX
            pick = group & (source % PC == kind * 8 + j)
            spread_ref[:, at : at + VOX] = jnp.where(pick, 1.0, 0.0).astype(BF16)
    for d in range(2):
        def body(k, carry):
            spot = spot_ref[d * KT + k]
            for a in range(NA):
                tile_at(found_ref, (d * NA + a) * KT + k)[...] = tile_at(image_ref, spot + a * XC)[...]
            return carry

        lax.fori_loop(0, KT, body, 0, unroll=8)
    clear(field_ref)


def fold(start, tiles_ref, traces):
    lane_in = iota((2 * VOX, VOX), 0) % VOX
    lane_out = iota((2 * VOX, VOX), 1)
    total = None
    for i in range(PR):
        pick = jnp.where((lane_out // PC == i) & (lane_out % PC == lane_in % PC), 1.0, 0.0).astype(BF16)
        rows = tiles_ref[pl.ds(start * PR + i, NA * KT, stride=PR), :] * traces
        high = rows.astype(BF16)
        low = (rows - high.astype(F32)).astype(BF16)
        part = jnp.dot(jnp.concatenate([high, low], axis=1), pick, preferred_element_type=F32)
        total = part if total is None else total + part
    return total


def renew(d, place_ref, rows_ref, found_ref, field_ref, trace_ref, rebuilt):
    def body(k, carry):
        base = place_ref[d * KT + k]
        for a in range(NA):
            tile_at(rebuilt, a * KT + k)[...] = tile_at(field_ref, base + a * XC)[...]
        return carry

    lax.fori_loop(0, KT, body, 0, unroll=8)
    traces = jnp.concatenate([trace_ref[d * KT : (d + 1) * KT, :]] * NA, axis=0)
    ratio = fold(d * NA * KT, found_ref, traces) / (fold(0, rebuilt, traces) + EPSILON)
    return (rows_ref[0 : NA * KT, :].astype(F32) * ratio).astype(BF16)


def lower_kernel(
    place_ref, packet_ref, tiles_ref, found_ref, old_ref, mine_ref, near_ref, far_ref, spread_ref, cleared_ref,
    trace_ref, field_ref, out_ref, rebuilt,
):
    even = even_tile()
    first = mine_ref[:ROWS, :] + far_ref[...]
    second = mine_ref[ROWS:, :] + near_ref[...]
    upper = jnp.where(even, second, first)
    lower = jnp.where(even, first, second)
    numer, denom = unpack(jnp.concatenate([upper, lower], axis=0), spread_ref[...])
    trace_ref[...] = old_ref[...] * numer / (denom + EPSILON)
    rebuild(place_ref, tiles_ref, trace_ref, field_ref)
    out_ref[...] = renew(1, place_ref, packet_ref, found_ref, field_ref, trace_ref, rebuilt)


def upper_kernel(place_ref, upper_ref, found_ref, field_ref, trace_ref, out_ref, sent_ref, rebuilt):
    value = renew(0, place_ref, upper_ref, found_ref, field_ref, trace_ref, rebuilt)
    out_ref[...] = value
    sent_ref[...] = value


def merge_kernel(odd_ref, upper_ref, lower_ref, upper_other, lower_other, out_ref, wide):
    odd = odd_ref[...] > 0
    for a in range(NA):
        rows = slice(a * KT, (a + 1) * KT)
        for d, mine_ref, other_ref in ((0, upper_ref, upper_other), (1, lower_ref, lower_other)):
            mine = mine_ref[rows, :].astype(F32)
            other = other_ref[rows, :].astype(F32)
            wide[pl.ds(4 * a + 2 * d, KT, stride=16), :] = jnp.where(odd, other, mine)
            wide[pl.ds(4 * a + 2 * d + 1, KT, stride=16), :] = jnp.where(odd, mine, other)
    out_ref[...] = wide[...].astype(BF16)


def shards(movie, shifts, footprints, blocks, traces, counts):
    tiles = lax.axis_size("tile")
    tile = lax.axis_index("tile")
    core = lax.axis_index("nrn")
    down = [(i, (i + 1) % tiles) for i in range(tiles)]
    up = [(j, i) for i, j in down]
    cross = [(0, 1), (1, 0)]

    def shape(rows, dtype):
        return jax.ShapeDtypeStruct((rows, VOX), dtype)

    mine = traces[0]
    above = lax.ppermute(mine, "tile", down)
    theirs = lax.ppermute(mine, "nrn", cross)

    hbm = pltpu.with_memory_space_constraint
    block_rows = hbm(blocks.T, pltpu.HBM)
    foot_rows = hbm(footprints.reshape(-1, VOX), pltpu.HBM)
    wide = pltpu.VMEM((KT * 16, VOX), F32)
    packet = call(
        rows_kernel, shape(NA * KT + KT, BF16), [smem(), vmem(), vmem()], scratch=[wide], name="rows", limit=4,
    )(counts, block_rows, foot_rows)
    packet_in = lax.ppermute(packet, "tile", down)

    height, width = movie.shape[2:]
    outside = pl.BlockSpec(memory_space=pltpu.HBM)
    sent = call(
        register_kernel, shape(tiles * 2 * XC, BF16), [smem(), outside],
        scratch=[
            pltpu.VMEM((height, width), BF16), pltpu.VMEM((tiles * 2 * XC, VOX), BF16),
            pltpu.SemaphoreType.DMA((5,)), pltpu.SemaphoreType.DMA((5,)),
        ],
        out_specs=outside, name="register", limit=12,
    )(hbm(shifts[0, 0], pltpu.HBM), hbm(movie[0, 0], pltpu.HBM))
    sent, packet_in, above, theirs = lax.optimization_barrier((sent, packet_in, above, theirs))
    images = lax.all_to_all(
        sent.reshape(tiles * 2, XC, VOX), ("tile", "nrn"), split_axis=0, concat_axis=0, tiled=True
    ).reshape(-1, VOX)

    upper, odd = call(
        own_rows_kernel, [pltpu.HBM((NA * KT, VOX), BF16), shape(KT, jnp.int32)],
        [smem(), vmem(), vmem(), pl.BlockSpec(memory_space=pl.ANY)], scratch=[wide], name="own_rows", limit=4,
    )(counts, block_rows, foot_rows, packet_in)

    both = jnp.concatenate([mine, above], axis=0)
    other = jnp.concatenate([theirs, lax.ppermute(above, "nrn", cross)], axis=0)
    frames = jnp.stack([jnp.where(core == 0, both, other), jnp.where(core == 0, other, both)], axis=-1)
    old = jnp.broadcast_to(frames.reshape(NH, NF)[:, :, None], (NH, NF, PC)).reshape(NH, VOX)

    def base_of(info):
        return info[NA * KT :, 0].astype(jnp.int32) * XC + info[NA * KT :, 64].astype(jnp.int32)

    base, base_in = base_of(packet), base_of(packet_in)
    margin = tile == 0
    place = jnp.concatenate([base, base_in + jnp.where(margin, FIELD, 0)])
    spot = jnp.concatenate([base, jnp.where(margin, FIELD, base_in)])

    field = pltpu.VMEM((2 * FIELD * PR, VOX), F32)
    sums = pltpu.VMEM((NH * PR, VOX), F32)
    in_vmem = pltpu.with_memory_space_constraint
    tiles_e = call(
        denom_kernel, pltpu.VMEM((TILES * PR + NH, VOX), F32), [smem()] + [vmem()] * 3,
        scratch=[field, sums], name="denominator", limit=14,
    )(place, upper, packet_in, old)
    tiles_e = in_vmem(tiles_e, pltpu.VMEM)
    image_field, partial = call(
        numer_kernel, [pltpu.VMEM(((FIELD + PADF) * PR, VOX), F32), shape(2 * ROWS, F32)],
        [smem(), vmem(), vmem()],
        scratch=[pltpu.VMEM((NF * VOX, NF * VOX), BF16), sums],
        name="numerator", limit=12,
    )(spot, tiles_e, in_vmem(images, pltpu.VMEM))
    image_field = in_vmem(image_field, pltpu.VMEM)

    partial = partial + lax.ppermute(partial, "nrn", cross)
    near = [(i, i ^ 1) for i in range(tiles)]
    far = [(i, (i - 1 + 2 * (i % 2)) % tiles) for i in range(tiles)]
    from_far = lax.ppermute(partial[:ROWS], "tile", far)
    from_near = lax.ppermute(partial[ROWS:], "tile", near)

    image_field, _ = lax.optimization_barrier((image_field, partial))
    found, cleared, spread = call(
        stage_kernel,
        [
            pltpu.VMEM((TILES * PR, VOX), F32), pltpu.VMEM((2 * FIELD * PR, VOX), F32),
            pltpu.VMEM((VOX, 2 * KT // ROWS * VOX), BF16),
        ],
        [smem(), vmem()], name="stage", limit=4,
    )(spot, in_vmem(image_field, pltpu.VMEM))
    found, cleared, spread = [in_vmem(v, pltpu.VMEM) for v in (found, cleared, spread)]
    half = pltpu.VMEM((NA * KT * PR, VOX), F32)
    new, rebuilt, lower_new = call(
        lower_kernel,
        [shape(NH, F32), pltpu.VMEM((2 * FIELD * PR, VOX), F32), shape(NA * KT, BF16)],
        [smem()] + [vmem()] * 9,
        scratch=[half], name="lower", limit=8, aliases={9: 1},
    )(place, packet_in, tiles_e, found, old, partial, from_near, from_far, spread, cleared)
    lower_back = lax.ppermute(lower_new, "tile", up)
    upper_new, upper_sent = call(
        upper_kernel, [shape(NA * KT, BF16)] * 2, [smem()] + [vmem()] * 4,
        scratch=[half], name="upper", limit=8,
    )(place, upper, found, in_vmem(rebuilt, pltpu.VMEM), new)
    upper_other = lax.ppermute(upper_sent, "nrn", cross)
    lower_other = lax.ppermute(lower_back, "nrn", cross)
    merged = call(
        merge_kernel, shape(KT * 16, BF16), [vmem()] * 5,
        scratch=[pltpu.VMEM((KT * 16, VOX), F32)], name="merge", limit=4,
    )(odd, upper_new, lower_back, upper_other, lower_other)

    frames_new = new[:KT].reshape(KT, NF, PC)[:, :, 0].reshape(KT, NF // 2, 2)
    updated = jnp.where(core == 0, frames_new[:, :, 0], frames_new[:, :, 1])
    return updated[None], merged.reshape(KT, 16, VOX)


def solution(mesh):
    placed = (
        P("nrn", "tile", None, None),
        P("nrn", "tile", None),
        P("tile", None, None),
        P("tile", None),
        P("nrn", "tile", None),
        P("tile"),
    )
    return jax.shard_map(
        shards,
        mesh=mesh,
        in_specs=placed,
        out_specs=(P("nrn", "tile", None), P("tile", None, None)),
        check_vma=False,
    )
```

```python
import jax
import jax.numpy as jnp
from jax import lax
from jax.experimental import pallas as pl
from jax.experimental.pallas import tpu as pltpu
from jax.sharding import PartitionSpec as P

Z = 32
PR = 8
PC = 16
VOX = PR * PC
ROWS = 16
CHUNKS = 2
BAND = 224
NF = 8
KT = 96
NH = 2 * KT
NA = 4
XC = 32
TILES = NA * NH
FIELD = Z * XC
PADF = 4 * XC
EPSILON = 1e-06
MIB = 1024 * 1024

F32 = jnp.float32
BF16 = jnp.bfloat16


def iota(shape, dim):
    return lax.broadcasted_iota(jnp.int32, shape, dim)


def vmem():
    return pl.BlockSpec(memory_space=pltpu.VMEM)


def smem():
    return pl.BlockSpec(memory_space=pltpu.SMEM)


def call(kernel, out_shape, in_specs, scratch=(), name=None, limit=24, out_specs=None, aliases=None):
    if out_specs is None:
        out_specs = [vmem() for _ in out_shape] if isinstance(out_shape, (list, tuple)) else vmem()
    return pl.pallas_call(
        kernel,
        out_shape=out_shape,
        in_specs=in_specs,
        out_specs=out_specs,
        scratch_shapes=list(scratch),
        input_output_aliases=aliases or {},
        compiler_params=pltpu.CompilerParams(vmem_limit_bytes=limit * MIB),
        name=name,
    )


def places(block_ref):
    first = block_ref[...]
    ones = jnp.where(iota((16, VOX), 0) == 0, 1.0, 0.0).astype(BF16)

    def down_rows(values):
        return lax.dot_general(
            values.astype(F32).astype(BF16), ones, (((0,), (0,)), ((), ())), preferred_element_type=F32
        )

    plane = down_rows(first // 128)
    column = down_rows(first % 64).astype(jnp.int32)
    odd = (column + lax.axis_index("nrn")) % 2
    return plane, (column + odd) // 2, odd


def pick_rows(d, count_ref, odd, foot_ref, out_ref, wide):
    wide[...] = foot_ref[...].astype(F32)
    live = iota((KT, VOX), 0) < count_ref[0]
    for a in range(NA):
        left = wide[pl.ds(4 * a + 2 * d, KT, stride=16), :]
        right = wide[pl.ds(4 * a + 2 * d + 1, KT, stride=16), :]
        value = jnp.where(live, jnp.where(odd > 0, right, left), 0.0)
        out_ref[a * KT : (a + 1) * KT, :] = value.astype(BF16)


def rows_kernel(count_ref, block_ref, foot_ref, packet_ref, wide):
    plane, place, odd = places(block_ref)
    info = jnp.where(iota((KT, VOX), 1) < 64, plane, place.astype(F32))
    packet_ref[NA * KT : NA * KT + KT, :] = info.astype(BF16)
    pick_rows(1, count_ref, odd, foot_ref, packet_ref, wide)


def own_rows_kernel(count_ref, block_ref, foot_ref, packet_ref, upper_ref, odd_ref, wide):
    odd = places(block_ref)[2]
    odd_ref[...] = odd
    pick_rows(0, count_ref, odd, foot_ref, upper_ref, wide)


def register_kernel(shift_ref, movie_ref, out_ref, image, laid, load_sem, store_sem):
    height, width = movie_ref.shape
    bands = [(lo, min(height, lo + BAND)) for lo in range(0, height, BAND)]
    edges = [0] + [min(height, hi + 16) for _, hi in bands]
    loads = []
    for b in range(len(bands)):
        rows = pl.ds(edges[b], edges[b + 1] - edges[b])
        loads.append(pltpu.make_async_copy(movie_ref.at[rows, :], image.at[rows, :], load_sem.at[b]))
        loads[-1].start()
    s = shift_ref[0]
    u = shift_ref[1]
    groups = width // 256
    src = iota((512, 256), 0) - 128
    lane = iota((512, 256), 1) % 128
    want_column = (lane // PC) * 32 + (iota((512, 256), 1) // 128) * PC + lane % PC
    pick = jnp.where(src == want_column - u, 1.0, 0.0).astype(BF16)
    stores = []
    for b, (first, last) in enumerate(bands):
        loads[b].wait()
        lo = max(0, first - 16)
        hi = min(height, last + 16)
        want = iota((last - first, hi - lo), 0) + first - s
        have = iota((last - first, hi - lo), 1) + lo
        move = jnp.where(want == have, 1.0, 0.0).astype(BF16)
        rows = jnp.dot(move, image[lo:hi, :], preferred_element_type=F32).astype(BF16)
        parts = []
        for g in range(groups):
            start = max(0, 256 * g - 128)
            stop = min(width, 256 * g + 384)
            part = pick[start - 256 * g + 128 : stop - 256 * g + 128, :]
            parts.append(jnp.dot(rows[:, start:stop], part, preferred_element_type=F32))
        for t in range((last - first) // PR):
            for c in range(2):
                piece = [p[t * PR : (t + 1) * PR, c * 128 : (c + 1) * 128] for p in parts]
                at = ((first // PR + t) * 2 + c) * groups * PR
                laid[at : at + groups * PR, :] = jnp.concatenate(piece, axis=0).astype(BF16)
        where = pl.ds(first * 2 * groups, (last - first) * 2 * groups)
        stores.append(pltpu.make_async_copy(laid.at[where, :], out_ref.at[where, :], store_sem.at[b]))
        stores[-1].start()
    for copy in stores:
        copy.wait()


def tile_at(ref, block):
    return ref.at[pl.ds(pl.multiple_of(block * PR, PR), PR), :]


def expand(upper_ref, lower_ref, tiles_ref):
    lane_in = iota((VOX, PR * VOX), 0)
    lane_out = iota((VOX, PR * VOX), 1)
    same = (lane_in // PC == lane_out // VOX) & (lane_in % PC == lane_out % PC)
    spread = jnp.where(same, 1.0, 0.0).astype(BF16)
    for a in range(NA):
        for d, ref in ((0, upper_ref), (1, lower_ref)):
            rows = ref[a * KT : (a + 1) * KT, :]
            wide = jnp.dot(rows, spread, preferred_element_type=F32)
            base = (a * NH + d * KT) * PR
            for i in range(PR):
                tiles_ref[pl.ds(base + i, KT, stride=PR), :] = wide[:, i * VOX : (i + 1) * VOX]


def zero(ref, start, rows):
    step = 256

    def body(k, carry):
        ref[pl.ds(pl.multiple_of(start + k * step, step), step), :] = jnp.zeros((step, VOX), F32)
        return carry

    lax.fori_loop(0, rows // step, body, 0)


def clear(field_ref):
    zero(field_ref, 0, FIELD * PR)

    @pl.when(lax.axis_index("tile") == 0)
    def _():
        zero(field_ref, FIELD * PR, FIELD * PR)


def rebuild(place_ref, tiles_ref, trace_ref, field_ref):
    def body(n, carry):
        trace = jnp.broadcast_to(trace_ref[pl.ds(n, 1), :], (PR, VOX))
        base = place_ref[n]
        held = [tile_at(field_ref, base + a * XC)[...] for a in range(NA)]
        added = [tile_at(tiles_ref, a * NH + n)[...] * trace for a in range(NA)]
        for a in range(NA):
            tile_at(field_ref, base + a * XC)[...] = held[a] + added[a]
        return carry

    lax.fori_loop(0, NH, body, 0, unroll=16)


def project(place_ref, tiles_ref, field_ref, sums_ref):
    def body(n, carry):
        base = place_ref[n]
        total = tile_at(tiles_ref, n)[...] * tile_at(field_ref, base)[...]
        for a in range(1, NA):
            total = total + tile_at(tiles_ref, a * NH + n)[...] * tile_at(field_ref, base + a * XC)[...]
        tile_at(sums_ref, n)[...] = total
        return carry

    lax.fori_loop(0, NH, body, 0, unroll=16)
    rows = sums_ref[pl.ds(0, NH, stride=PR), :]
    for i in range(1, PR):
        rows = rows + sums_ref[pl.ds(i, NH, stride=PR), :]
    group = jnp.where(iota((VOX, VOX), 0) // PC == iota((VOX, VOX), 1) // PC, 1.0, 0.0)
    return jnp.dot(rows, group, preferred_element_type=F32, precision=lax.Precision.HIGHEST)


def denom_kernel(
    place_ref, upper_ref, packet_ref, trace_ref, tiles_ref, field, sums
):
    expand(upper_ref, packet_ref, tiles_ref)
    clear(field)
    rebuild(place_ref, tiles_ref, trace_ref, field)
    tiles_ref[TILES * PR : TILES * PR + NH, :] = project(place_ref, tiles_ref, field, sums)


def pack(rows):
    slot = iota((ROWS, VOX), 1) % 8
    packed = jnp.zeros((ROWS, VOX), F32)
    for j in range(KT // ROWS):
        packed = jnp.where(slot == j, rows[j * ROWS : (j + 1) * ROWS, :], packed)
    return packed


def unpack(packed, spread):
    high = packed.astype(BF16)
    rest = packed - high.astype(F32)
    middle = rest.astype(BF16)
    low = (rest - middle.astype(F32)).astype(BF16)
    wide = jnp.dot(jnp.concatenate([high, middle, low], axis=0), spread, preferred_element_type=F32)
    wide = wide[: 2 * ROWS] + wide[2 * ROWS : 4 * ROWS] + wide[4 * ROWS :]
    slots = KT // ROWS
    parts = []
    for kind in range(2):
        rows = []
        for d in range(2):
            for j in range(slots):
                at = (kind * slots + j) * VOX
                rows.append(wide[d * ROWS : (d + 1) * ROWS, at : at + VOX])
        parts.append(jnp.concatenate(rows, axis=0))
    return parts


def even_tile():
    return lax.bitwise_and(lax.axis_index("tile"), 1) == 0


def numer_kernel(place_ref, tiles_ref, image_ref, field_ref, sums_ref, permute_ref, sums):
    groups = XC // 8
    rows = groups * PR
    step = Z // CHUNKS
    chunk = step * NF * rows
    source = iota((VOX, NF * VOX), 0)
    target = iota((VOX, NF * VOX), 1)
    same = (source // PC == target // VOX) & (source % PC == target % PC)
    same = jnp.where(same, 1.0, 0.0).astype(BF16)
    frame = iota((16, NF * VOX), 1) % VOX // PC
    for f in range(NF):
        mine = jnp.where(frame == f, 1.0, 0.0).astype(BF16)
        for r in range(VOX // 16):
            at = f * VOX + 16 * r
            permute_ref[at : at + 16, :] = same[16 * r : 16 * r + 16, :] * mine
    for k in range(CHUNKS):
        lhs = []
        for z in range(step):
            start = k * chunk + z * NF * rows
            frames = [image_ref[start + f * rows : start + (f + 1) * rows, :] for f in range(NF)]
            lhs.append(jnp.concatenate(frames, axis=1))
        out = jnp.dot(jnp.concatenate(lhs, axis=0), permute_ref[...], preferred_element_type=F32)
        for z in range(step):
            for g in range(groups):
                for x in range(8):
                    at = z * rows + g * PR
                    to = ((k * step + z) * XC + g * 8 + x) * PR
                    field_ref[to : to + PR, :] = out[at : at + PR, x * VOX : (x + 1) * VOX]
    field_ref[FIELD * PR : (FIELD + PADF) * PR, :] = jnp.zeros((PADF * PR, VOX), F32)
    numer = project(place_ref, tiles_ref, field_ref, sums)
    denom = tiles_ref[TILES * PR : TILES * PR + NH, :]
    value = jnp.where(iota((NH, VOX), 1) % PC < PC // 2, numer, denom)
    upper, lower = pack(value[:KT, :]), pack(value[KT:, :])
    even = even_tile()
    sums_ref[:ROWS, :] = jnp.where(even, lower, upper)
    sums_ref[ROWS:, :] = jnp.where(even, upper, lower)


def stage_kernel(spot_ref, image_ref, found_ref, field_ref, spread_ref):
    source = iota((VOX, VOX), 0)
    group = source // PC == iota((VOX, VOX), 1) // PC
    slots = KT // ROWS
    for kind in range(2):
        for j in range(slots):
            at = (kind * slots + j) * VOX
            pick = group & (source % PC == kind * 8 + j)
            spread_ref[:, at : at + VOX] = jnp.where(pick, 1.0, 0.0).astype(BF16)
    for d in range(2):
        def body(k, carry):
            spot = spot_ref[d * KT + k]
            for a in range(NA):
                tile_at(found_ref, (d * NA + a) * KT + k)[...] = tile_at(image_ref, spot + a * XC)[...]
            return carry

        lax.fori_loop(0, KT, body, 0, unroll=16)
    clear(field_ref)


def fold(start, tiles_ref, traces):
    lane_in = iota((2 * VOX, VOX), 0) % VOX
    lane_out = iota((2 * VOX, VOX), 1)
    total = None
    for i in range(PR):
        pick = jnp.where((lane_out // PC == i) & (lane_out % PC == lane_in % PC), 1.0, 0.0).astype(BF16)
        rows = tiles_ref[pl.ds(start * PR + i, NA * KT, stride=PR), :] * traces
        high = rows.astype(BF16)
        low = (rows - high.astype(F32)).astype(BF16)
        part = jnp.dot(jnp.concatenate([high, low], axis=1), pick, preferred_element_type=F32)
        total = part if total is None else total + part
    return total


def renew(d, place_ref, rows_ref, found_ref, field_ref, trace_ref, rebuilt):
    def body(k, carry):
        base = place_ref[d * KT + k]
        for a in range(NA):
            tile_at(rebuilt, a * KT + k)[...] = tile_at(field_ref, base + a * XC)[...]
        return carry

    lax.fori_loop(0, KT, body, 0, unroll=16)
    traces = jnp.concatenate([trace_ref[d * KT : (d + 1) * KT, :]] * NA, axis=0)
    ratio = fold(d * NA * KT, found_ref, traces) / (fold(0, rebuilt, traces) + EPSILON)
    return (rows_ref[0 : NA * KT, :].astype(F32) * ratio).astype(BF16)


def lower_kernel(
    place_ref, packet_ref, tiles_ref, found_ref, old_ref, mine_ref, near_ref, far_ref, spread_ref, cleared_ref,
    trace_ref, field_ref, out_ref, rebuilt,
):
    even = even_tile()
    first = mine_ref[:ROWS, :] + far_ref[...]
    second = mine_ref[ROWS:, :] + near_ref[...]
    upper = jnp.where(even, second, first)
    lower = jnp.where(even, first, second)
    numer, denom = unpack(jnp.concatenate([upper, lower], axis=0), spread_ref[...])
    trace_ref[...] = old_ref[...] * numer / (denom + EPSILON)
    rebuild(place_ref, tiles_ref, trace_ref, field_ref)
    out_ref[...] = renew(1, place_ref, packet_ref, found_ref, field_ref, trace_ref, rebuilt)


def upper_kernel(place_ref, upper_ref, found_ref, field_ref, trace_ref, out_ref, sent_ref, rebuilt):
    value = renew(0, place_ref, upper_ref, found_ref, field_ref, trace_ref, rebuilt)
    out_ref[...] = value
    sent_ref[...] = value


def merge_kernel(odd_ref, upper_ref, lower_ref, upper_other, lower_other, out_ref, wide):
    odd = odd_ref[...] > 0
    for a in range(NA):
        rows = slice(a * KT, (a + 1) * KT)
        for d, mine_ref, other_ref in ((0, upper_ref, upper_other), (1, lower_ref, lower_other)):
            mine = mine_ref[rows, :].astype(F32)
            other = other_ref[rows, :].astype(F32)
            wide[pl.ds(4 * a + 2 * d, KT, stride=16), :] = jnp.where(odd, other, mine)
            wide[pl.ds(4 * a + 2 * d + 1, KT, stride=16), :] = jnp.where(odd, mine, other)
    out_ref[...] = wide[...].astype(BF16)


def shards(movie, shifts, footprints, blocks, traces, counts):
    tiles = lax.axis_size("tile")
    tile = lax.axis_index("tile")
    core = lax.axis_index("nrn")
    down = [(i, (i + 1) % tiles) for i in range(tiles)]
    up = [(j, i) for i, j in down]
    cross = [(0, 1), (1, 0)]

    def shape(rows, dtype):
        return jax.ShapeDtypeStruct((rows, VOX), dtype)

    mine = traces[0]
    above = lax.ppermute(mine, "tile", down)
    theirs = lax.ppermute(mine, "nrn", cross)

    hbm = pltpu.with_memory_space_constraint
    block_rows = hbm(blocks.T, pltpu.HBM)
    foot_rows = hbm(footprints.reshape(-1, VOX), pltpu.HBM)
    wide = pltpu.VMEM((KT * 16, VOX), F32)
    packet = call(
        rows_kernel, shape(NA * KT + KT, BF16), [smem(), vmem(), vmem()], scratch=[wide], name="rows", limit=4,
    )(counts, block_rows, foot_rows)
    packet_in = lax.ppermute(packet, "tile", down)

    height, width = movie.shape[2:]
    outside = pl.BlockSpec(memory_space=pltpu.HBM)
    sent = call(
        register_kernel, shape(tiles * 2 * XC, BF16), [smem(), outside],
        scratch=[
            pltpu.VMEM((height, width), BF16), pltpu.VMEM((tiles * 2 * XC, VOX), BF16),
            pltpu.SemaphoreType.DMA((5,)), pltpu.SemaphoreType.DMA((5,)),
        ],
        out_specs=outside, name="register", limit=12,
    )(hbm(shifts[0, 0], pltpu.HBM), hbm(movie[0, 0], pltpu.HBM))
    sent, packet_in, above, theirs = lax.optimization_barrier((sent, packet_in, above, theirs))
    images = lax.all_to_all(
        sent.reshape(tiles * 2, XC, VOX), ("tile", "nrn"), split_axis=0, concat_axis=0, tiled=True
    ).reshape(-1, VOX)

    upper, odd = call(
        own_rows_kernel, [pltpu.HBM((NA * KT, VOX), BF16), shape(KT, jnp.int32)],
        [smem(), vmem(), vmem(), pl.BlockSpec(memory_space=pl.ANY)], scratch=[wide], name="own_rows", limit=4,
    )(counts, block_rows, foot_rows, packet_in)

    both = jnp.concatenate([mine, above], axis=0)
    other = jnp.concatenate([theirs, lax.ppermute(above, "nrn", cross)], axis=0)
    frames = jnp.stack([jnp.where(core == 0, both, other), jnp.where(core == 0, other, both)], axis=-1)
    old = jnp.broadcast_to(frames.reshape(NH, NF)[:, :, None], (NH, NF, PC)).reshape(NH, VOX)

    def base_of(info):
        return info[NA * KT :, 0].astype(jnp.int32) * XC + info[NA * KT :, 64].astype(jnp.int32)

    base, base_in = base_of(packet), base_of(packet_in)
    margin = tile == 0
    place = jnp.concatenate([base, base_in + jnp.where(margin, FIELD, 0)])
    spot = jnp.concatenate([base, jnp.where(margin, FIELD, base_in)])

    field = pltpu.VMEM((2 * FIELD * PR, VOX), F32)
    sums = pltpu.VMEM((NH * PR, VOX), F32)
    in_vmem = pltpu.with_memory_space_constraint
    tiles_e = call(
        denom_kernel, pltpu.VMEM((TILES * PR + NH, VOX), F32), [smem()] + [vmem()] * 3,
        scratch=[field, sums], name="denominator", limit=14,
    )(place, upper, packet_in, old)
    tiles_e = in_vmem(tiles_e, pltpu.VMEM)
    image_field, partial = call(
        numer_kernel, [pltpu.VMEM(((FIELD + PADF) * PR, VOX), F32), shape(2 * ROWS, F32)],
        [smem(), vmem(), vmem()],
        scratch=[pltpu.VMEM((NF * VOX, NF * VOX), BF16), sums],
        name="numerator", limit=12,
    )(spot, tiles_e, in_vmem(images, pltpu.VMEM))
    image_field = in_vmem(image_field, pltpu.VMEM)

    everyone = ("tile", "nrn")

    def other_core(pairs):
        return [(2 * i + c, 2 * j + 1 - c) for i, j in pairs for c in (0, 1)]

    partial = partial + lax.ppermute(partial, "nrn", cross)
    near = [(i, i ^ 1) for i in range(tiles)]
    far = [(i, (i - 1 + 2 * (i % 2)) % tiles) for i in range(tiles)]
    from_far = lax.ppermute(partial[:ROWS], "tile", far)
    from_near = lax.ppermute(partial[ROWS:], "tile", near)

    image_field, _ = lax.optimization_barrier((image_field, partial))
    found, cleared, spread = call(
        stage_kernel,
        [
            pltpu.VMEM((TILES * PR, VOX), F32), pltpu.VMEM((2 * FIELD * PR, VOX), F32),
            pltpu.VMEM((VOX, 2 * KT // ROWS * VOX), BF16),
        ],
        [smem(), vmem()], name="stage", limit=4,
    )(spot, in_vmem(image_field, pltpu.VMEM))
    found, cleared, spread = [in_vmem(v, pltpu.VMEM) for v in (found, cleared, spread)]
    half = pltpu.VMEM((NA * KT * PR, VOX), F32)
    new, rebuilt, lower_new = call(
        lower_kernel,
        [shape(NH, F32), pltpu.VMEM((2 * FIELD * PR, VOX), F32), shape(NA * KT, BF16)],
        [smem()] + [vmem()] * 9,
        scratch=[half], name="lower", limit=8, aliases={9: 1},
    )(place, packet_in, tiles_e, found, old, partial, from_near, from_far, spread, cleared)
    lower_back = lax.ppermute(lower_new, "tile", up)
    lower_other = lax.ppermute(lower_new, everyone, other_core(up))
    upper_new, upper_sent = call(
        upper_kernel, [shape(NA * KT, BF16)] * 2, [smem()] + [vmem()] * 4,
        scratch=[half], name="upper", limit=8,
    )(place, upper, found, in_vmem(rebuilt, pltpu.VMEM), new)
    upper_other = lax.ppermute(upper_sent, "nrn", cross)
    merged = call(
        merge_kernel, shape(KT * 16, BF16), [vmem()] * 5,
        scratch=[pltpu.VMEM((KT * 16, VOX), F32)], name="merge", limit=4,
    )(odd, upper_new, lower_back, upper_other, lower_other)

    frames_new = new[:KT].reshape(KT, NF, PC)[:, :, 0].reshape(KT, NF // 2, 2)
    updated = jnp.where(core == 0, frames_new[:, :, 0], frames_new[:, :, 1])
    return updated[None], merged.reshape(KT, 16, VOX)


def solution(mesh):
    placed = (
        P("nrn", "tile", None, None),
        P("nrn", "tile", None),
        P("tile", None, None),
        P("tile", None),
        P("nrn", "tile", None),
        P("tile"),
    )
    return jax.shard_map(
        shards,
        mesh=mesh,
        in_specs=placed,
        out_specs=(P("nrn", "tile", None), P("tile", None, None)),
        check_vma=False,
    )
```
